128 devices in a mesh: seq: 32 (over x, y, core), head: 4 (over z).
Axes of the slice: x: 4, y: 4, z: 4, core: 2. Of those that a mesh axis runs over, the one named last changes fastest.
Arguments:
- tokens: bfloat16 [8192, 2560], P(('seq', 'head')), may hold values from -6 to 6
- input_gain: float32 [2560], replicated, may hold values from 0.5 to 1.5
- gate_weight: bfloat16 [2560, 5120], P(None, 'head'), may hold values from -0.125 to 0.125
- inner_weight: bfloat16 [2560, 5120], P(None, 'head'), may hold values from -0.125 to 0.125
- state_weight: bfloat16 [2560, 256], replicated, may hold values from -0.125 to 0.125
- step_weight: bfloat16 [2560, 80], P(None, 'head'), may hold values from -0.125 to 0.125
- step_bias: float32 [80], P('head'), may hold values from -1 to 1
- decay_exponent: int32 [80], P('head'), may hold values from 64 to 65024
- conv_inner: float32 [4, 5120], P(None, 'head'), may hold values from -3 to 3
- conv_state: float32 [4, 256], replicated, may hold values from -3 to 3
- skip_gain: float32 [80], P('head'), may hold values from 0.5 to 1.5
- norm_gain: float32 [5120], P('head'), may hold values from 0.5 to 1.5
- out_weight: bfloat16 [5120, 2560], P('head'), may hold values from -0.078125 to 0.078125
- passage_lengths: int32 [64], replicated, may hold values from 1 to 4096, 8192 in all
Outputs:
- mixed: bfloat16 [8192, 2560], P(('seq', 'head'))
The draws below stay inside these ranges and needn't reach their ends.
Inputs may be any that keep to these rules, and one draw needn't show every extreme that they name: `passage_lengths`: the 64 passages lie end to end and fill all 8192 tokens; the longest has exactly 4096 tokens.
All inputs are finite; a program needn't handle non-finite values.
Results may differ from the reference program's by a relative error of at most 0.017.
Values may be sent and summed in bfloat16 or wider, within the bound.
No kernel may reach another device: no remote copies, remote signals or barrier semaphores. Data moves between devices by JAX's collectives and lax.ppermute only.
A program may use at most 128 MiB of HBM per device.

```python
import math
import jax
import jax.numpy as jnp
import numpy as np
from jax import lax

D = 2560
H = 80
P_SIZE = 64
N = 128
K = 4
Q = 256
TOKENS = 8192
PASSAGES = 64
LONGEST = 4096


def draw_decay_exponent(key, part):
    keys = jax.random.split(key, 3)
    mantissa = jax.random.randint(keys[0], (H,), 64, 128)
    power = jax.random.randint(keys[1], (H,), 0, 10)
    values = jnp.left_shift(mantissa, power)
    order = jax.random.permutation(keys[2], H)
    slots = jnp.arange(H)
    values = jnp.where(slots == order[0], 64, values)
    values = jnp.where(slots == order[1], 65024, values)
    return values.astype(jnp.int32)


def shard_levels(key, dims, cuts, smallest, high):
    def one(position, parts):
        draws = jax.random.uniform(jax.random.fold_in(jax.random.fold_in(key, 6), position), (parts,), jnp.float32, smallest / len(cuts), high / len(cuts))
        return jnp.repeat(jnp.exp(draws), dims[position] // parts).reshape((-1,) + (1,) * (len(dims) - position - 1))

    factor_of = one(*cuts[0])
    for cut in cuts[1:]:
        factor_of = factor_of * one(*cut)
    return factor_of


def profile(amount, total, limit, lean):
    portions = [(1 << 20) // math.isqrt(grade ** lean) + 1 for grade in range(2, amount + 1)]
    surplus, given = total - limit - (amount - 1), [1] * (amount - 1)
    while surplus > 0:
        movable = [i for i in range(amount - 1) if given[i] < limit]
        mass, left = sum([portions[i] for i in movable]), surplus
        for i in movable:
            more = min(limit - given[i], max(1, left * portions[i] // mass), surplus)
            given[i] = given[i] + more
            surplus = surplus - more
    return np.array([limit] + given)


def ragged(key, amount, total, reach, lean):
    if amount == 2:
        one = jax.random.randint(key, (), max(1, total - reach), min(reach, total - 1) + 1)
        return jnp.stack([one, total - one])
    sizes = jnp.asarray(profile(amount, total, reach, lean), jnp.int32)
    pairs = (amount - 1) // 2
    giver, taker = sizes[1:1 + 2 * pairs:2], sizes[2:2 + 2 * pairs:2]
    room = jnp.minimum(giver - 1, reach - taker)
    moved = jax.random.randint(jax.random.fold_in(key, 1), (pairs,), 0, 1 << 20) % (room + 1)
    sizes = sizes.at[1:1 + 2 * pairs:2].set(giver - moved).at[2:2 + 2 * pairs:2].set(taker + moved)
    return sizes[jax.random.permutation(jax.random.fold_in(key, 2), amount)]


def bell_draw(rng, shape, spread, most, cuts=(), kind=jnp.bfloat16):
    array = jax.random.normal(rng, shape, jnp.float32) * spread
    if len(cuts) > 0:
        array = shard_levels(rng, shape, cuts, -0.22, 0.18) * array
    return jnp.clip(array, min=-most, max=most).astype(kind)


def setup_inputs(seed: int = 0) -> dict:
    arg_keys = jax.random.split(jax.random.key(seed), 15)
    return {
        "tokens": bell_draw(arg_keys[0], (TOKENS, D), 1.0, 6.0, ((0, 128),)),
        "input_gain": jnp.clip(1.0 + 0.1 * jax.random.normal(arg_keys[1], (D,), jnp.float32), 0.5, 1.5),
        "gate_weight": bell_draw(arg_keys[2], (D, H * P_SIZE), D ** -0.5, 0.125, ((1, 4),)),
        "inner_weight": bell_draw(arg_keys[3], (D, H * P_SIZE), D ** -0.5, 0.125, ((1, 4),)),
        "state_weight": bell_draw(arg_keys[4], (D, 2 * N), D ** -0.5, 0.125),
        "step_weight": bell_draw(arg_keys[5], (D, H), D ** -0.5, 0.125, ((1, 4),)),
        "step_bias": jnp.clip(jax.random.uniform(arg_keys[6], (H,), jnp.float32, -1.0, 1.0) * shard_levels(arg_keys[6], (H,), ((0, 4),), -0.4, 0.0), -1.0, 1.0),
        "decay_exponent": draw_decay_exponent(jax.random.fold_in(arg_keys[14], 71), 0),
        "conv_inner": bell_draw(arg_keys[8], (K, H * P_SIZE), 0.5, 3.0, ((1, 4),), jnp.float32),
        "conv_state": bell_draw(arg_keys[9], (K, 2 * N), 0.5, 3.0, (), jnp.float32),
        "skip_gain": jnp.clip(0.5 + 1.0 * jax.random.uniform(arg_keys[10], (H,), jnp.float32) ** shard_levels(arg_keys[10], (H,), ((0, 4),), -0.2, 0.2), 0.5, 1.5),
        "norm_gain": jnp.clip(1.0 + 0.1 * jax.random.normal(arg_keys[11], (H * P_SIZE,), jnp.float32), 0.5, 1.5),
        "out_weight": bell_draw(arg_keys[12], (H * P_SIZE, D), (H * P_SIZE) ** -0.5, 0.078125, ((0, 4),)),
        "passage_lengths": ragged(arg_keys[13], PASSAGES, TOKENS, LONGEST, 2).astype(jnp.int32),
    }


PRECISE = lax.Precision.HIGHEST

def passage_ids(lengths, positions):
    starts = jnp.cumsum(lengths) - lengths
    return lax.optimization_barrier(jnp.sum((positions[:, None] >= starts[None, :]).astype(jnp.int32), axis=1)) - 1

def causal_conv(padded, weights, ids, padded_ids):
    length = ids.shape[0]
    total = jnp.zeros((length, padded.shape[1]), jnp.float32)
    for offset in range(K):
        first = K - 1 - offset
        shifted = padded[first:first + length]
        agrees = (padded_ids[first:first + length] == ids).astype(jnp.float32)
        total = total + weights[offset][None, :] * shifted * agrees[:, None]
    return jax.nn.silu(total)

def ssd_group(state, block):
    inner_part, step_part, log_part, in_part, out_part, ids_part, prev_id = block
    cumulative = jnp.cumsum(log_part, axis=0)
    count = ids_part.shape[0]
    order = jnp.arange(count)
    pairs_mask = (ids_part[:, None] == ids_part[None, :]) & (order[:, None] >= order[None, :])
    cum_heads = cumulative.T
    gaps = cum_heads[:, :, None] - cum_heads[:, None, :]
    decay_mat = jnp.exp(jnp.where(pairs_mask[None, :, :], gaps, -1e+30))
    scores = jnp.dot(out_part, in_part.T, preferred_element_type=jnp.float32)
    weighted = (decay_mat * scores[None, :, :]).astype(jnp.bfloat16)
    scaled_in = (inner_part.astype(jnp.float32) * step_part[:, :, None]).transpose(1, 0, 2).astype(jnp.bfloat16)
    intra = jnp.einsum('hts,hsp->htp', weighted, scaled_in, preferred_element_type=jnp.float32).transpose(1, 0, 2)
    keep_first = (ids_part == prev_id).astype(jnp.float32)
    decay_first = jnp.exp(cumulative) * keep_first[:, None]
    inter = jnp.einsum('tn,hnp->thp', out_part.astype(jnp.float32), state, precision=PRECISE) * decay_first[:, :, None]
    tail_decay = jnp.exp(cumulative[-1][None, :] - cumulative) * (ids_part == ids_part[-1]).astype(jnp.float32)[:, None]
    carry_keep = jnp.exp(cumulative[-1]) * (ids_part[-1] == prev_id).astype(jnp.float32)
    tail_in = (tail_decay.T[:, :, None] * scaled_in.astype(jnp.float32)).astype(jnp.bfloat16)
    new_state = state * carry_keep[:, None, None] + jnp.einsum('sn,hsp->hnp', in_part, tail_in, preferred_element_type=jnp.float32)
    return (new_state, intra + inter)

def reference(tokens, input_gain, gate_weight, inner_weight, state_weight, step_weight, step_bias, decay_exponent, conv_inner, conv_state, skip_gain, norm_gain, out_weight, passage_lengths):
    tok_float = tokens.astype(jnp.float32)
    normed = (tok_float * lax.rsqrt(lax.optimization_barrier(jnp.mean(tok_float * tok_float, axis=-1, keepdims=True)) + 1e-05) * input_gain).astype(jnp.bfloat16)
    gate_vals = jnp.dot(normed, gate_weight, preferred_element_type=jnp.float32).astype(jnp.bfloat16)
    inner_raw = jnp.dot(normed, inner_weight, preferred_element_type=jnp.float32).astype(jnp.bfloat16)
    state_raw = jnp.dot(normed, state_weight, preferred_element_type=jnp.float32).astype(jnp.bfloat16)
    step_raw = jnp.dot(normed, step_weight, preferred_element_type=jnp.float32)
    length = tokens.shape[0]
    positions = jnp.arange(length, dtype=jnp.int32)
    ids = passage_ids(passage_lengths, positions)
    padded_ids = jnp.concatenate([jnp.full((K - 1,), -1, jnp.int32), ids])
    inner_pad = jnp.concatenate([jnp.zeros((K - 1, inner_raw.shape[1]), jnp.float32), inner_raw.astype(jnp.float32)])
    state_pad = jnp.concatenate([jnp.zeros((K - 1, state_raw.shape[1]), jnp.float32), state_raw.astype(jnp.float32)])
    inner_conv = causal_conv(inner_pad, conv_inner, ids, padded_ids).astype(jnp.bfloat16)
    state_conv = causal_conv(state_pad, conv_state, ids, padded_ids).astype(jnp.bfloat16)
    state_in = state_conv[:, :N]
    state_out = state_conv[:, N:]
    step_size = jax.nn.softplus(step_raw + step_bias)
    log_decay = -step_size * (decay_exponent.astype(jnp.float32) * 2.0 ** (-21))
    groups = length // Q
    heads_x = inner_conv.reshape(length, H, P_SIZE)
    id_groups = ids.reshape(groups, Q)
    prev_ids = jnp.concatenate([jnp.full((1,), -1, jnp.int32), id_groups[:-1, -1]])
    start_state = jnp.zeros((H, N, P_SIZE), jnp.float32)
    blocks = (heads_x.reshape(groups, Q, H, P_SIZE), step_size.reshape(groups, Q, H), log_decay.reshape(groups, Q, H), state_in.reshape(groups, Q, N), state_out.reshape(groups, Q, N), id_groups, prev_ids)
    final_state, pieces = lax.scan(ssd_group, start_state, blocks)
    ssd_out = pieces.reshape(length, H, P_SIZE) + skip_gain[None, :, None] * heads_x.astype(jnp.float32)
    gated = ssd_out.reshape(length, H * P_SIZE) * jax.nn.silu(gate_vals.astype(jnp.float32))
    normed_out = (gated * lax.rsqrt(lax.optimization_barrier(jnp.mean(gated * gated, axis=-1, keepdims=True)) + 1e-05) * norm_gain).astype(jnp.bfloat16)
    return jnp.dot(normed_out, out_weight, preferred_element_type=jnp.float32).astype(jnp.bfloat16)
```

```python
import jax
import jax.numpy as jnp
from jax import lax
from jax.sharding import PartitionSpec as P

H = 80
P_SIZE = 64
N = 128
K = 4
RIM = 8
LANES = 128


def from_behind(block, axis, distance):
    devices = range(lax.axis_size(axis))
    route = [(i - distance, i) for i in devices if i - distance in devices]
    return lax.ppermute(block, axis, route)


def around(block, axis, distance):
    size = lax.axis_size(axis)
    return lax.ppermute(block, axis, [(i, (i + distance) % size) for i in range(size)])


def gather_tokens(tokens):
    size = lax.axis_size("head")
    here = lax.axis_index("head")
    rows = tokens.shape[0]
    whole = jnp.zeros((size * rows, tokens.shape[1]), tokens.dtype)
    whole = lax.dynamic_update_slice(whole, tokens, (here * rows, 0))
    for distance in range(1, size):
        piece = around(tokens, "head", distance)
        owner = (here - distance) % size
        whole = lax.dynamic_update_slice(whole, piece, (owner * rows, 0))
    return whole


def gather_rim(tokens):
    heads = lax.axis_size("head")
    blocks = lax.axis_size("seq")
    tail = tokens[tokens.shape[0] - RIM :]
    total = None
    for target in range(heads):
        route = [
            (s * heads + heads - 1, (s + 1) * heads + target) for s in range(blocks - 1)
        ]
        piece = lax.ppermute(tail, ("seq", "head"), route)
        total = piece if total is None else total + piece
    return total


def split3(x):
    first = x.astype(jnp.bfloat16)
    rest = x - first.astype(jnp.float32)
    second = rest.astype(jnp.bfloat16)
    third = (rest - second.astype(jnp.float32)).astype(jnp.bfloat16)
    return first, second, third


def passage_ids(lengths, positions):
    starts = jnp.cumsum(lengths) - lengths
    return jnp.sum((positions[:, None] >= starts[None, :]).astype(jnp.int32), axis=1) - 1


def causal_conv(padded, weights, ids, padded_ids):
    length = ids.shape[0]
    total = jnp.zeros((length, padded.shape[1]), jnp.float32)
    for offset in range(K):
        first = RIM - offset
        shifted = padded[first : first + length]
        agrees = (padded_ids[first : first + length] == ids).astype(jnp.float32)
        total = total + weights[offset][None, :] * shifted * agrees[:, None]
    return jax.nn.silu(total)


def spread(x):
    return jnp.repeat(x, P_SIZE, axis=1)


def carried_states(local, total_decay):
    blocks = lax.axis_size("seq")
    heads_here = total_decay.shape[0]
    parts = jnp.concatenate(split3(total_decay))
    parts = jnp.pad(parts, (0, LANES - parts.shape[0]))
    sent = jnp.concatenate(
        [local.astype(jnp.bfloat16), jnp.broadcast_to(parts[None], (N, LANES))], axis=1
    )
    got = lax.all_to_all(sent, "seq", 0, 0, tiled=True)
    width = local.shape[1]
    pieces = got[:, :width].astype(jnp.float32).reshape(blocks, N // blocks, width)
    decays = got[:, width:].astype(jnp.float32).reshape(blocks, N // blocks, LANES)[:, 0]
    decays = sum(decays[:, i * heads_here : (i + 1) * heads_here] for i in range(3))
    decays = spread(decays)
    state = jnp.zeros((N // blocks, width), jnp.float32)
    outs = []
    for b in range(blocks):
        outs.append(state)
        state = decays[b][None] * state + pieces[b]
    back = jnp.stack(outs).astype(jnp.bfloat16).reshape(N, width)
    return lax.all_to_all(back, "seq", 0, 0, tiled=True)


def on_device(
    tokens,
    input_gain,
    gate_weight,
    inner_weight,
    state_weight,
    step_weight,
    step_bias,
    decay_exponent,
    conv_inner,
    conv_state,
    skip_gain,
    norm_gain,
    out_weight,
    passage_lengths,
):
    rows = tokens.shape[0]
    whole = jnp.concatenate([gather_rim(tokens), gather_tokens(tokens)])
    length = whole.shape[0] - RIM
    tok_float = whole.astype(jnp.float32)
    normed = (
        tok_float
        * lax.rsqrt(jnp.mean(tok_float * tok_float, axis=-1, keepdims=True) + 1e-05)
        * input_gain
    ).astype(jnp.bfloat16)
    gate_vals = jnp.dot(normed[RIM:], gate_weight, preferred_element_type=jnp.float32).astype(
        jnp.bfloat16
    )
    inner_pad = jnp.dot(normed, inner_weight, preferred_element_type=jnp.float32).astype(
        jnp.bfloat16
    )
    state_pad = jnp.dot(normed, state_weight, preferred_element_type=jnp.float32).astype(
        jnp.bfloat16
    )
    step_raw = jnp.dot(normed[RIM:], step_weight, preferred_element_type=jnp.float32)
    heads_here = step_weight.shape[1]
    first_pos = lax.axis_index("seq") * length
    padded_pos = first_pos + jnp.arange(-RIM, length, dtype=jnp.int32)
    padded_ids = passage_ids(passage_lengths, padded_pos)
    ids = padded_ids[RIM:]
    prior_id = padded_ids[RIM - 1]
    inner_conv = causal_conv(
        inner_pad.astype(jnp.float32), conv_inner, ids, padded_ids
    ).astype(jnp.bfloat16)
    state_conv = causal_conv(
        state_pad.astype(jnp.float32), conv_state, ids, padded_ids
    ).astype(jnp.bfloat16)
    state_in = state_conv[:, :N]
    state_out = state_conv[:, N:]
    step_size = jax.nn.softplus(step_raw + step_bias)
    log_decay = -step_size * (decay_exponent.astype(jnp.float32) * 2.0 ** (-21))
    cum = jnp.cumsum(log_decay, axis=0)
    tail = jnp.exp(cum[-1][None] - cum) * (ids == ids[-1]).astype(jnp.float32)[:, None]
    head_decay = jnp.exp(cum) * (ids == prior_id).astype(jnp.float32)[:, None]
    conv_float = inner_conv.astype(jnp.float32)
    scaled_in = (conv_float * spread(step_size)).astype(jnp.bfloat16)
    tail_in = (spread(tail) * scaled_in.astype(jnp.float32)).astype(jnp.bfloat16)
    local = jnp.dot(state_in.T, tail_in, preferred_element_type=jnp.float32)
    incoming = carried_states(local, head_decay[-1])

    order = jnp.arange(length)
    mask = (ids[:, None] == ids[None, :]) & (order[:, None] >= order[None, :])
    scores = jnp.dot(state_out, state_in.T, preferred_element_type=jnp.float32)
    cum_heads = cum.T
    gaps = cum_heads[:, :, None] - cum_heads[:, None, :]
    decay_mat = jnp.exp(jnp.where(mask[None], gaps, -1e30))
    weighted = (decay_mat * scores[None]).astype(jnp.bfloat16)
    intra = jnp.einsum(
        "hts,shp->thp",
        weighted,
        scaled_in.reshape(length, heads_here, P_SIZE),
        preferred_element_type=jnp.float32,
    ).reshape(length, heads_here * P_SIZE)
    inter = jnp.dot(state_out, incoming, preferred_element_type=jnp.float32) * spread(head_decay)
    ssd_out = intra + inter + spread(skip_gain[None]) * conv_float
    gated = ssd_out * jax.nn.silu(gate_vals.astype(jnp.float32))
    squares = jnp.sum(gated * gated, axis=1, keepdims=True)
    partial = jnp.dot(
        (gated * norm_gain).astype(jnp.bfloat16), out_weight, preferred_element_type=jnp.float32
    )
    sent = jnp.concatenate(
        [partial.astype(jnp.bfloat16), jnp.pad(jnp.concatenate(split3(squares), 1), ((0, 0), (0, LANES - 3)))],
        axis=1,
    )
    here = lax.axis_index("head")
    size = lax.axis_size("head")
    pieces = [lax.dynamic_slice_in_dim(sent, here * rows, rows)]
    for distance in range(1, size):
        target = (here + distance) % size
        pieces.append(
            around(lax.dynamic_slice_in_dim(sent, target * rows, rows), "head", distance)
        )
    total = sum(p.astype(jnp.float32) for p in pieces)
    width = partial.shape[1]
    mean = jnp.sum(total[:, width : width + 3], axis=1, keepdims=True) / (H * P_SIZE)
    return (total[:, :width] * lax.rsqrt(mean + 1e-05)).astype(jnp.bfloat16)


def solution(mesh):
    in_specs = (
        P(("seq", "head"), None),
        P(),
        P(None, "head"),
        P(None, "head"),
        P(),
        P(None, "head"),
        P("head"),
        P("head"),
        P(None, "head"),
        P(),
        P("head"),
        P("head"),
        P("head", None),
        P(),
    )
    out_specs = P(("seq", "head"), None)
    return jax.shard_map(
        on_device, mesh=mesh, in_specs=in_specs, out_specs=out_specs, check_vma=False
    )
```

```python
import jax
import jax.numpy as jnp
from jax import lax
from jax.experimental import pallas as pl
from jax.experimental.pallas import tpu as pltpu
from jax.sharding import PartitionSpec as P

H = 80
P_SIZE = 64
N = 128
K = 4
RIM = 16
LANES = 128
CHUNK = 256
WIDE = 512
VMEM_LIMIT = 40 << 20
F32 = jnp.float32
BF16 = jnp.bfloat16


def around(block, axis, distance):
    size = lax.axis_size(axis)
    return lax.ppermute(block, axis, [(i, (i + distance) % size) for i in range(size)])


def gather_tokens(tokens):
    heads = lax.axis_size("head")
    blocks = lax.axis_size("seq")
    half = tokens.shape[0] // 2
    tail = tokens[tokens.shape[0] - RIM :]
    below = around(tokens, "head", 1)
    above = around(tokens, "head", heads - 1)
    rim = None
    for target in range(0, heads, 2):
        route = [
            (s * heads + heads - 1, (s + 1) * heads + target) for s in range(blocks - 1)
        ]
        piece = lax.ppermute(tail, ("seq", "head"), route)
        rim = piece if rim is None else rim + piece
    top = around(jnp.concatenate([below[:half], rim]), "head", 1)
    bottom = around(above[half:], "head", heads - 1)
    return below, above, top, bottom, rim


def split3(x):
    first = x.astype(BF16).astype(F32)
    rest = x - first
    second = rest.astype(BF16).astype(F32)
    return first, second, rest - second


def by_lane(x, count):
    lane = lax.broadcasted_iota(jnp.int32, x.shape, 1)
    first, second, third = split3(x)
    picked = jnp.where(lane < count, first, jnp.where(lane < 2 * count, second, third))
    return jnp.where(lane < 3 * count, picked, 0.0).astype(BF16)


def head_slot(shape, count):
    slot = lax.broadcasted_iota(jnp.int32, shape, 0)
    live = slot < 3 * count
    slot = slot - jnp.where(slot >= 2 * count, 2 * count, jnp.where(slot >= count, count, 0))
    return jnp.where(live, slot, -1)


def spread_matrix(first_head, width, count):
    shape = (LANES, width)
    head = first_head + lax.broadcasted_iota(jnp.int32, shape, 1) // P_SIZE
    return jnp.where(head_slot(shape, count) == head, 1.0, 0.0).astype(BF16)


def dot(a, b):
    return jnp.dot(a, b, preferred_element_type=F32)


def block_kernel(
    place,
    lens_row,
    lens_col,
    own,
    below,
    above,
    top,
    bottom,
    rim,
    gain,
    state_w,
    step_w,
    step_bias,
    rate,
    taps_state,
    inner_w,
    taps_inner,
    normed_out,
    sent,
    conv_out,
    scaled_out,
    cum_out,
    cum_rows,
    scores_out,
    maps_out,
    head_decay_out,
    normed,
    agree,
    step3,
    tail3,
    maps_in_t,
    local,
    total3,
    *,
    heads_here,
):
    j = pl.program_id(0)
    rows = own.shape[0]
    length = normed.shape[0] - RIM

    def conv(raw, taps):
        acc = taps[0:1, :] * raw[RIM:]
        for lag in range(1, K):
            moved = pltpu.roll(raw, lag, 0)[RIM:]
            same = agree[lag - 1]
            same = jnp.concatenate([same] * (raw.shape[1] // LANES), axis=1)
            acc = acc + taps[lag : lag + 1, :] * moved * same
        return (acc * jax.nn.sigmoid(acc)).astype(BF16)

    @pl.when(j == 0)
    def _():
        here = place[0]
        first = place[1]

        def norm(x):
            x = x.astype(F32)
            mean = jnp.mean(x * x, axis=-1, keepdims=True)
            return (x * lax.rsqrt(mean + 1e-05) * gain[...]).astype(BF16)

        def put(owner, offset, x):
            start = pl.multiple_of(RIM + owner * rows + offset, RIM)
            normed[pl.ds(start, x.shape[0]), :] = norm(x)

        half = rows // 2
        put(here, 0, own[...])
        put((here + 3) % 4, 0, below[...])
        put((here + 1) % 4, 0, above[...])
        far = (here + 2) % 4
        put(far, 0, top[0:half, :])
        put(far, half, bottom[...])
        rim_tokens = (rim[...].astype(F32) + top[half:, :].astype(F32)).astype(BF16)
        normed[0:RIM, :] = norm(rim_tokens)
        normed_out[...] = normed[RIM:, :]

        passages = lens_row.shape[1]
        up = lax.broadcasted_iota(jnp.int32, (passages, passages), 0)
        across = lax.broadcasted_iota(jnp.int32, (passages, passages), 1)
        starts_row = jnp.sum(
            jnp.where(up < across, lens_col[...].astype(F32), 0.0), axis=0, keepdims=True
        )
        starts_col = jnp.sum(
            jnp.where(across < up, lens_row[...].astype(F32), 0.0), axis=1, keepdims=True
        )
        base = first.astype(F32)
        pos = lax.broadcasted_iota(jnp.int32, (length + RIM, passages), 0).astype(F32)
        ids_pad = jnp.sum(
            jnp.where(pos + (base - RIM) >= starts_row, 1.0, 0.0), axis=1, keepdims=True
        )
        pos = lax.broadcasted_iota(jnp.int32, (passages, length), 1).astype(F32)
        ids_row = jnp.sum(jnp.where(pos + base >= starts_col, 1.0, 0.0), axis=0, keepdims=True)
        ids_wide = jnp.broadcast_to(ids_pad, (length + RIM, LANES))
        ids = ids_wide[RIM:]
        for lag in range(1, K):
            agree[lag - 1] = jnp.where(pltpu.roll(ids_wide, lag, 0)[RIM:] == ids, 1.0, 0.0)

        raw = dot(normed[...], state_w[...]).astype(BF16).astype(F32)
        maps = conv(raw, taps_state)
        maps_in = maps[:, :N]
        maps_out[...] = maps[:, N:]
        maps_in_t[...] = maps_in.astype(F32).T.astype(BF16)
        t = lax.broadcasted_iota(jnp.int32, (length, length), 0)
        s = lax.broadcasted_iota(jnp.int32, (length, length), 1)
        ids_two = jnp.concatenate([ids] * (length // LANES), axis=1)
        mask = (ids_two == ids_row) & (t >= s)
        scores_out[...] = jnp.where(mask, dot(maps[:, N:], maps_in_t[...]), 0.0)

        x = dot(normed[RIM:, :], step_w[...]) + step_bias[...]
        step = jnp.maximum(x, 0.0) + jnp.log1p(jnp.exp(-jnp.abs(x)))
        log_decay = -step * rate[...]
        ones = jnp.where(t >= s, 1.0, 0.0).astype(BF16)
        cum = sum(dot(ones, part.astype(BF16)) for part in split3(log_decay))
        last = cum[length - 1 :, :]
        ids_last = ids[length - 1 :, :]
        prior = ids_wide[RIM - 1 : RIM, :]
        step3[...] = by_lane(step, heads_here)
        tail = jnp.exp(jnp.minimum(last - cum, 0.0)) * jnp.where(ids == ids_last, 1.0, 0.0)
        tail3[...] = by_lane(tail, heads_here)
        keep = jnp.exp(cum) * jnp.where(ids == prior, 1.0, 0.0)
        head_decay_out[...] = by_lane(keep, heads_here)
        total3[...] = by_lane(keep, heads_here)[length - RIM :].astype(F32)
        cum_out[...] = by_lane(cum, heads_here)
        cum_rows[...] = cum.T

    raw = dot(normed[...], inner_w[...]).astype(BF16).astype(F32)
    mixed = conv(raw, taps_inner)
    conv_out[...] = mixed
    spread = spread_matrix(j * (CHUNK // P_SIZE), CHUNK, heads_here)
    scaled = (mixed.astype(F32) * dot(step3[...], spread)).astype(BF16)
    scaled_out[...] = scaled
    tail_in = (dot(tail3[...], spread) * scaled.astype(F32)).astype(BF16)
    local[:, pl.ds(pl.multiple_of(j * CHUNK, CHUNK), CHUNK)] = dot(maps_in_t[...], tail_in)

    @pl.when(j == pl.num_programs(0) - 1)
    def _():
        span = local.shape[1] // 2
        decay = jnp.broadcast_to(total3[RIM - 1 : RIM, :], (8, LANES)).astype(BF16)
        for piece in range(sent.shape[0]):
            group, side = piece // 2, piece % 2
            block = local[8 * group : 8 * group + 8, side * span : (side + 1) * span]
            sent[piece, :, 0:span] = block.astype(BF16)
            sent[piece, :, span:] = decay


def inside_kernel(
    normed, gate_w, scaled, conv, cum, cum_rows, scores, skip, inside, gate, *, heads_here
):
    j = pl.program_id(0)
    length = scaled.shape[0]
    half = length // 2
    per = CHUNK // P_SIZE
    lane = lax.broadcasted_iota(jnp.int32, scaled.shape, 1) // P_SIZE
    slots = head_slot((LANES, length), heads_here)
    x = scaled[...]
    tops, bottoms, top_x, all_x = [], [], [], []
    for i in range(per):
        head = j * per + i
        pick = jnp.where(slots == head, 1.0, 0.0).astype(BF16)
        cum_t = dot(cum[...], pick)
        cum_s = cum_rows[pl.ds(head, 1), :]
        own = jnp.where(lane == i, x, jnp.zeros_like(x))
        upper = jnp.exp(jnp.minimum(cum_t[:half, :half] - cum_s[:, :half], 0.0))
        lower = jnp.exp(jnp.minimum(cum_t[half:] - cum_s, 0.0))
        tops.append((upper * scores[0:half, 0:half]).astype(BF16))
        bottoms.append((lower * scores[half:, :]).astype(BF16))
        top_x.append(own[:half])
        all_x.append(own)
    upper = dot(jnp.concatenate(tops, axis=1), jnp.concatenate(top_x, axis=0))
    lower = dot(jnp.concatenate(bottoms, axis=1), jnp.concatenate(all_x, axis=0))
    inside[...] = jnp.concatenate([upper, lower], axis=0) + skip[...] * conv[...].astype(F32)
    vals = dot(normed[...], gate_w[...]).astype(BF16).astype(F32)
    gate[...] = vals * jax.nn.sigmoid(vals)


def scan_kernel(place, got, back, *, heads_here):
    blocks, depth, width = got.shape
    span = width - LANES
    side = place[0] % 2
    spread = spread_matrix(side * (span // P_SIZE), span, heads_here)
    parts = got[:, :, span:].astype(F32).reshape(blocks * depth, LANES).astype(BF16)
    decay = dot(parts, spread)
    state = jnp.zeros((depth, span), F32)
    for b in range(blocks):
        back[b] = state.astype(BF16)
        if b < blocks - 1:
            state = decay[b * depth : (b + 1) * depth] * state + got[b, :, 0:span].astype(F32)


def out_kernel(
    place,
    got,
    maps,
    head_decay,
    inside,
    gate,
    norm_gain,
    out_w,
    out0,
    out1,
    out2,
    out3,
    states,
    x,
    sums,
    *,
    heads_here,
):
    j = pl.program_id(0)
    outs = (out0, out1, out2, out3)
    length = inside.shape[0]
    rows = length // 4
    width = out_w.shape[1] * pl.num_programs(0)

    @pl.when(j == 0)
    def _():
        here = place[0]
        span = got.shape[2]
        for piece in range(got.shape[0]):
            group, side = piece // 2, piece % 2
            states[8 * group : 8 * group + 8, side * span : (side + 1) * span] = got[
                piece
            ].astype(F32)
        total = jnp.zeros((length, 1), F32)
        for c in range(inside.shape[1] // CHUNK):
            cols = slice(c * CHUNK, (c + 1) * CHUNK)
            spread = spread_matrix(c * (CHUNK // P_SIZE), CHUNK, heads_here)
            carried = dot(maps[...], states[:, cols].astype(BF16)) * dot(head_decay[...], spread)
            gated = (inside[:, cols] + carried) * gate[:, cols]
            total = total + jnp.sum(gated * gated, axis=1, keepdims=True)
            ready = (gated * norm_gain[:, cols]).astype(BF16)
            for b in range(4):
                start = pl.multiple_of(((b + 4 - here) % 4) * rows, rows)
                x[pl.ds(start, rows), cols] = ready[b * rows : (b + 1) * rows]
        packed = by_lane(jnp.broadcast_to(total, (length, LANES)), 1)
        for b in range(4):
            start = pl.multiple_of(((b + 4 - here) % 4) * rows, rows)
            sums[pl.ds(start, rows), :] = packed[b * rows : (b + 1) * rows]
        for d in range(4):
            outs[d][:, 5 * WIDE :] = sums[d * rows : (d + 1) * rows, :]

    part = dot(x[...], out_w[...]).astype(BF16)
    for d in range(4):
        start = pl.multiple_of(j * WIDE, WIDE)
        outs[d][:, pl.ds(start, WIDE)] = part[d * rows : (d + 1) * rows]


def whole(shape):
    return pl.BlockSpec(shape, lambda j: (0,) * len(shape))


def columns(shape):
    return pl.BlockSpec(shape, lambda j: (0, j))


def smem():
    return pl.BlockSpec(memory_space=pltpu.SMEM)


def params():
    return pltpu.CompilerParams(
        dimension_semantics=("arbitrary",), vmem_limit_bytes=VMEM_LIMIT
    )


def on_device(
    tokens,
    input_gain,
    gate_weight,
    inner_weight,
    state_weight,
    step_weight,
    step_bias,
    decay_exponent,
    conv_inner,
    conv_state,
    skip_gain,
    norm_gain,
    out_weight,
    passage_lengths,
):
    rows, width = tokens.shape
    heads = lax.axis_size("head")
    blocks = lax.axis_size("seq")
    heads_here = step_weight.shape[1]
    channels = heads_here * P_SIZE
    length = heads * rows
    passages = passage_lengths.shape[0]
    span = channels // 2
    steps = channels // CHUNK
    here = lax.axis_index("head")
    block = lax.axis_index("seq")
    place = jnp.stack([here, block * length]).astype(jnp.int32)

    def lanes3(a):
        a = jnp.concatenate([a] * 3, axis=-1)
        return jnp.pad(a, ((0, 0), (0, LANES - a.shape[1])))

    step_w = lanes3(step_weight)
    bias = lanes3(step_bias[None])
    rate = lanes3(decay_exponent.astype(F32)[None] * 2.0 ** (-21))
    skip = jnp.repeat(skip_gain, P_SIZE)[None]
    below, above, top, bottom, rim = gather_tokens(tokens)

    def shape(dims, kind):
        return jax.ShapeDtypeStruct(dims, kind)

    half = rows // 2
    normed, sent, conv, scaled, cum, cum_rows, scores, maps, head_decay = pl.pallas_call(
        lambda *refs: block_kernel(*refs, heads_here=heads_here),
        grid=(steps,),
        in_specs=[
            smem(),
            whole((1, passages)),
            whole((passages, 1)),
            whole((rows, width)),
            whole((rows, width)),
            whole((rows, width)),
            whole((half + RIM, width)),
            whole((half, width)),
            whole((RIM, width)),
            whole((1, width)),
            whole((width, 2 * N)),
            whole((width, LANES)),
            whole((1, LANES)),
            whole((1, LANES)),
            whole((K, 2 * N)),
            columns((width, CHUNK)),
            columns((K, CHUNK)),
        ],
        out_specs=[
            whole((length, width)),
            whole((blocks, 8, span + LANES)),
            columns((length, CHUNK)),
            columns((length, CHUNK)),
            whole((length, LANES)),
            whole((LANES, length)),
            whole((length, length)),
            whole((length, N)),
            whole((length, LANES)),
        ],
        out_shape=[
            shape((length, width), BF16),
            shape((blocks, 8, span + LANES), BF16),
            shape((length, channels), BF16),
            shape((length, channels), BF16),
            shape((length, LANES), BF16),
            shape((LANES, length), F32),
            shape((length, length), F32),
            shape((length, N), BF16),
            shape((length, LANES), BF16),
        ],
        scratch_shapes=[
            pltpu.VMEM((length + RIM, width), BF16),
            pltpu.VMEM((K - 1, length, LANES), F32),
            pltpu.VMEM((length, LANES), BF16),
            pltpu.VMEM((length, LANES), BF16),
            pltpu.VMEM((N, length), BF16),
            pltpu.VMEM((N, channels), F32),
            pltpu.VMEM((RIM, LANES), F32),
        ],
        compiler_params=params(),
        name="block",
    )(
        place,
        passage_lengths[None],
        passage_lengths[:, None],
        tokens,
        below,
        above,
        top,
        bottom,
        rim,
        input_gain[None],
        state_weight,
        step_w,
        bias,
        rate,
        conv_state,
        inner_weight,
        conv_inner,
    )

    got = lax.all_to_all(sent, "seq", 0, 0, tiled=True)
    inside, gate = pl.pallas_call(
        lambda *refs: inside_kernel(*refs, heads_here=heads_here),
        grid=(steps,),
        in_specs=[
            whole((length, width)),
            columns((width, CHUNK)),
            columns((length, CHUNK)),
            columns((length, CHUNK)),
            whole((length, LANES)),
            whole((LANES, length)),
            whole((length, length)),
            columns((1, CHUNK)),
        ],
        out_specs=[columns((length, CHUNK)), columns((length, CHUNK))],
        out_shape=[shape((length, channels), F32), shape((length, channels), F32)],
        compiler_params=params(),
        name="inside",
    )(normed, gate_weight, scaled, conv, cum, cum_rows, scores, skip)

    back = pl.pallas_call(
        lambda *refs: scan_kernel(*refs, heads_here=heads_here),
        in_specs=[smem(), pl.BlockSpec(memory_space=pltpu.VMEM)],
        out_specs=pl.BlockSpec(memory_space=pltpu.VMEM),
        out_shape=shape((blocks, 8, span), BF16),
        compiler_params=pltpu.CompilerParams(vmem_limit_bytes=VMEM_LIMIT),
        name="scan",
    )(block.astype(jnp.int32)[None], got)
    states = lax.all_to_all(back, "seq", 0, 0, tiled=True)

    out_width = out_weight.shape[1]
    parts = pl.pallas_call(
        lambda *refs: out_kernel(*refs, heads_here=heads_here),
        grid=(out_width // WIDE,),
        in_specs=[
            smem(),
            whole((blocks, 8, span)),
            whole((length, N)),
            whole((length, LANES)),
            whole((length, channels)),
            whole((length, channels)),
            whole((1, channels)),
            columns((channels, WIDE)),
        ],
        out_specs=[whole((rows, out_width + LANES))] * 4,
        out_shape=[shape((rows, out_width + LANES), BF16)] * 4,
        scratch_shapes=[
            pltpu.VMEM((N, channels), F32),
            pltpu.VMEM((length, channels), BF16),
            pltpu.VMEM((length, LANES), BF16),
        ],
        compiler_params=params(),
        name="out",
    )(place, states, maps, head_decay, inside, gate, norm_gain[None], out_weight)
    total = parts[0].astype(F32)
    for distance in range(1, heads):
        total = total + around(parts[distance], "head", distance).astype(F32)
    mean = jnp.sum(total[:, out_width : out_width + 3], axis=1, keepdims=True) / (H * P_SIZE)
    return (total[:, :out_width] * lax.rsqrt(mean + 1e-05)).astype(BF16)


def solution(mesh):
    in_specs = (
        P(("seq", "head"), None),
        P(),
        P(None, "head"),
        P(None, "head"),
        P(),
        P(None, "head"),
        P("head"),
        P("head"),
        P(None, "head"),
        P(),
        P("head"),
        P("head"),
        P("head", None),
        P(),
    )
    out_specs = P(("seq", "head"), None)
    return jax.shard_map(
        on_device, mesh=mesh, in_specs=in_specs, out_specs=out_specs, check_vma=False
    )
```

```python
import jax
import jax.numpy as jnp
from jax import lax
from jax.experimental import pallas as pl
from jax.experimental.pallas import tpu as pltpu
from jax.sharding import PartitionSpec as P

H = 80
P_SIZE = 64
N = 128
K = 4
RIM = 16
LANES = 128
CHUNK = 256
WIDE = 512
VMEM_LIMIT = 60 << 20
F32 = jnp.float32
BF16 = jnp.bfloat16


def around(block, axis, distance):
    size = lax.axis_size(axis)
    return lax.ppermute(block, axis, [(i, (i + distance) % size) for i in range(size)])


def gather_tokens(tokens):
    heads = lax.axis_size("head")
    blocks = lax.axis_size("seq")
    half = tokens.shape[0] // 2
    tail = tokens[tokens.shape[0] - RIM :]
    below = around(tokens, "head", 1)
    above = around(tokens, "head", heads - 1)
    rim = None
    for target in range(2):
        route = [
            (s * heads + heads - 1, (s + 1) * heads + target) for s in range(blocks - 1)
        ]
        piece = lax.ppermute(tail, ("seq", "head"), route)
        rim = piece if rim is None else rim + piece
    top = around(tokens[:half], "head", 2)
    bottom = around(jnp.concatenate([tokens[half:], rim]), "head", 2)
    return below, above, top, bottom, rim


def far_memory(x):
    return pltpu.with_memory_space_constraint(x, pltpu.HBM)


def split3(x):
    first = x.astype(BF16).astype(F32)
    rest = x - first
    second = rest.astype(BF16).astype(F32)
    return first, second, rest - second


def by_lane(x, count):
    lane = lax.broadcasted_iota(jnp.int32, x.shape, 1)
    first, second, third = split3(x)
    picked = jnp.where(lane < count, first, jnp.where(lane < 2 * count, second, third))
    return jnp.where(lane < 3 * count, picked, 0.0).astype(BF16)


def head_slot(shape, count):
    slot = lax.broadcasted_iota(jnp.int32, shape, 0)
    live = slot < 3 * count
    slot = slot - jnp.where(slot >= 2 * count, 2 * count, jnp.where(slot >= count, count, 0))
    return jnp.where(live, slot, -1)


def spread_matrix(first_head, width, count):
    shape = (LANES, width)
    head = first_head + lax.broadcasted_iota(jnp.int32, shape, 1) // P_SIZE
    return jnp.where(head_slot(shape, count) == head, 1.0, 0.0).astype(BF16)


def dot(a, b):
    return jnp.dot(a, b, preferred_element_type=F32)


def block_kernel(
    place,
    lens_row,
    lens_col,
    own,
    below,
    above,
    top,
    bottom,
    rim,
    gain,
    state_w,
    step_w,
    step_bias,
    rate,
    taps_state,
    inner_w,
    taps_inner,
    normed_out,
    sent,
    conv_out,
    scaled_out,
    cum_out,
    cum_rows,
    scores_out,
    maps_out,
    head_decay_out,
    normed,
    agree,
    step3,
    tail3,
    maps_in_t,
    local,
    total3,
    *,
    heads_here,
):
    j = pl.program_id(0)
    rows = own.shape[0]
    length = normed.shape[0] - RIM

    def conv(raw, taps):
        acc = taps[0:1, :] * raw[RIM:]
        for lag in range(1, K):
            moved = pltpu.roll(raw, lag, 0)[RIM:]
            same = agree[lag - 1]
            same = jnp.concatenate([same] * (raw.shape[1] // LANES), axis=1)
            acc = acc + taps[lag : lag + 1, :] * moved * same
        return (acc * jax.nn.sigmoid(acc)).astype(BF16)

    @pl.when(j == 0)
    def _():
        here = place[0]
        first = place[1]

        def norm(x):
            x = x.astype(F32)
            mean = jnp.mean(x * x, axis=-1, keepdims=True)
            return (x * lax.rsqrt(mean + 1e-05) * gain[...]).astype(BF16)

        def put(owner, offset, x):
            start = pl.multiple_of(RIM + owner * rows + offset, RIM)
            normed[pl.ds(start, x.shape[0]), :] = norm(x)

        half = rows // 2
        put(here, 0, own[...])
        put((here + 3) % 4, 0, below[...])
        put((here + 1) % 4, 0, above[...])
        far = (here + 2) % 4
        put(far, 0, top[...])
        put(far, half, bottom[0:half, :])
        rim_tokens = (rim[...].astype(F32) + bottom[half:, :].astype(F32)).astype(BF16)
        normed[0:RIM, :] = norm(rim_tokens)
        normed_out[...] = normed[RIM:, :]

        passages = lens_row.shape[1]
        up = lax.broadcasted_iota(jnp.int32, (passages, passages), 0)
        across = lax.broadcasted_iota(jnp.int32, (passages, passages), 1)
        starts_row = jnp.sum(
            jnp.where(up < across, lens_col[...].astype(F32), 0.0), axis=0, keepdims=True
        )
        starts_col = jnp.sum(
            jnp.where(across < up, lens_row[...].astype(F32), 0.0), axis=1, keepdims=True
        )
        base = first.astype(F32)
        pos = lax.broadcasted_iota(jnp.int32, (length + RIM, passages), 0).astype(F32)
        ids_pad = jnp.sum(
            jnp.where(pos + (base - RIM) >= starts_row, 1.0, 0.0), axis=1, keepdims=True
        )
        pos = lax.broadcasted_iota(jnp.int32, (passages, length), 1).astype(F32)
        ids_row = jnp.sum(jnp.where(pos + base >= starts_col, 1.0, 0.0), axis=0, keepdims=True)
        ids_wide = jnp.broadcast_to(ids_pad, (length + RIM, LANES))
        ids = ids_wide[RIM:]
        for lag in range(1, K):
            agree[lag - 1] = jnp.where(pltpu.roll(ids_wide, lag, 0)[RIM:] == ids, 1.0, 0.0)

        raw = dot(normed[...], state_w[...]).astype(BF16).astype(F32)
        maps = conv(raw, taps_state)
        maps_in = maps[:, :N]
        maps_out[...] = maps[:, N:]
        maps_in_t[...] = maps_in.astype(F32).T.astype(BF16)
        t = lax.broadcasted_iota(jnp.int32, (length, length), 0)
        s = lax.broadcasted_iota(jnp.int32, (length, length), 1)
        ids_two = jnp.concatenate([ids] * (length // LANES), axis=1)
        mask = (ids_two == ids_row) & (t >= s)
        scores_out[...] = jnp.where(mask, dot(maps[:, N:], maps_in_t[...]), 0.0)

        x = dot(normed[RIM:, :], step_w[...]) + step_bias[...]
        step = jnp.maximum(x, 0.0) + jnp.log1p(jnp.exp(-jnp.abs(x)))
        log_decay = -step * rate[...]
        ones = jnp.where(t >= s, 1.0, 0.0).astype(BF16)
        cum = sum(dot(ones, part.astype(BF16)) for part in split3(log_decay))
        last = cum[length - 1 :, :]
        ids_last = ids[length - 1 :, :]
        prior = ids_wide[RIM - 1 : RIM, :]
        step3[...] = by_lane(step, heads_here)
        tail = jnp.exp(jnp.minimum(last - cum, 0.0)) * jnp.where(ids == ids_last, 1.0, 0.0)
        tail3[...] = by_lane(tail, heads_here)
        keep = jnp.exp(cum) * jnp.where(ids == prior, 1.0, 0.0)
        head_decay_out[...] = by_lane(keep, heads_here)
        total3[...] = by_lane(keep, heads_here)[length - RIM :].astype(F32)
        cum_out[...] = by_lane(cum, heads_here)
        cum_rows[...] = cum.T

    raw = dot(normed[...], inner_w[...]).astype(BF16).astype(F32)
    mixed = conv(raw, taps_inner)
    conv_out[...] = mixed
    spread = spread_matrix(j * (CHUNK // P_SIZE), CHUNK, heads_here)
    scaled = (mixed.astype(F32) * dot(step3[...], spread)).astype(BF16)
    scaled_out[...] = scaled
    tail_in = (dot(tail3[...], spread) * scaled.astype(F32)).astype(BF16)
    local[:, pl.ds(pl.multiple_of(j * CHUNK, CHUNK), CHUNK)] = dot(maps_in_t[...], tail_in)

    @pl.when(j == pl.num_programs(0) - 1)
    def _():
        span = local.shape[1] // 2
        decay = jnp.broadcast_to(total3[RIM - 1 : RIM, :], (8, LANES)).astype(BF16)
        for piece in range(sent.shape[0]):
            group, side = piece // 2, piece % 2
            block = local[8 * group : 8 * group + 8, side * span : (side + 1) * span]
            sent[piece, :, 0:span] = block.astype(BF16)
            sent[piece, :, span:] = decay


def inside_kernel(
    normed, gate_w, scaled, conv, cum, cum_rows, scores, skip, inside, gate, *, heads_here
):
    j = pl.program_id(0)
    length = scaled.shape[0]
    half = length // 2
    per = CHUNK // P_SIZE
    lane = lax.broadcasted_iota(jnp.int32, scaled.shape, 1) // P_SIZE
    slots = head_slot((LANES, length), heads_here)
    x = scaled[...]
    tops, bottoms, top_x, all_x = [], [], [], []
    for i in range(per):
        head = j * per + i
        pick = jnp.where(slots == head, 1.0, 0.0).astype(BF16)
        cum_t = dot(cum[...], pick)
        cum_s = cum_rows[pl.ds(head, 1), :]
        own = jnp.where(lane == i, x, jnp.zeros_like(x))
        upper = jnp.exp(jnp.minimum(cum_t[:half, :half] - cum_s[:, :half], 0.0))
        lower = jnp.exp(jnp.minimum(cum_t[half:] - cum_s, 0.0))
        tops.append((upper * scores[0:half, 0:half]).astype(BF16))
        bottoms.append((lower * scores[half:, :]).astype(BF16))
        top_x.append(own[:half])
        all_x.append(own)
    upper = dot(jnp.concatenate(tops, axis=1), jnp.concatenate(top_x, axis=0))
    lower = dot(jnp.concatenate(bottoms, axis=1), jnp.concatenate(all_x, axis=0))
    inside[...] = jnp.concatenate([upper, lower], axis=0) + skip[...] * conv[...].astype(F32)
    vals = dot(normed[...], gate_w[...]).astype(BF16).astype(F32)
    gate[...] = vals * jax.nn.sigmoid(vals)


def scan_kernel(place, got, back, *, heads_here):
    blocks, depth, width = got.shape
    span = width - LANES
    side = place[0] % 2
    spread = spread_matrix(side * (span // P_SIZE), span, heads_here)
    parts = got[:, :, span:].astype(F32).reshape(blocks * depth, LANES).astype(BF16)
    decay = dot(parts, spread)
    state = jnp.zeros((depth, span), F32)
    for b in range(blocks):
        back[b] = state.astype(BF16)
        if b < blocks - 1:
            state = decay[b * depth : (b + 1) * depth] * state + got[b, :, 0:span].astype(F32)


def out_kernel(
    place,
    got,
    maps,
    head_decay,
    inside,
    gate,
    norm_gain,
    out_w,
    out0,
    out1,
    out2,
    out3,
    states,
    x,
    sums,
    *,
    heads_here,
):
    j = pl.program_id(0)
    outs = (out0, out1, out2, out3)
    length = inside.shape[0]
    rows = length // 4
    width = out_w.shape[1] * pl.num_programs(0)

    @pl.when(j == 0)
    def _():
        here = place[0]
        span = got.shape[2]
        for piece in range(got.shape[0]):
            group, side = piece // 2, piece % 2
            states[8 * group : 8 * group + 8, side * span : (side + 1) * span] = got[
                piece
            ].astype(F32)
        total = jnp.zeros((length, 1), F32)
        for c in range(inside.shape[1] // CHUNK):
            cols = slice(c * CHUNK, (c + 1) * CHUNK)
            spread = spread_matrix(c * (CHUNK // P_SIZE), CHUNK, heads_here)
            carried = dot(maps[...], states[:, cols].astype(BF16)) * dot(head_decay[...], spread)
            gated = (inside[:, cols] + carried) * gate[:, cols]
            total = total + jnp.sum(gated * gated, axis=1, keepdims=True)
            ready = (gated * norm_gain[:, cols]).astype(BF16)
            for b in range(4):
                start = pl.multiple_of(((b + 4 - here) % 4) * rows, rows)
                x[pl.ds(start, rows), cols] = ready[b * rows : (b + 1) * rows]
        packed = by_lane(jnp.broadcast_to(total, (length, LANES)), 1)
        for b in range(4):
            start = pl.multiple_of(((b + 4 - here) % 4) * rows, rows)
            sums[pl.ds(start, rows), :] = packed[b * rows : (b + 1) * rows]
        for d in range(4):
            outs[d][:, 5 * WIDE :] = sums[d * rows : (d + 1) * rows, :]

    part = dot(x[...], out_w[...]).astype(BF16)
    for d in range(4):
        start = pl.multiple_of(j * WIDE, WIDE)
        outs[d][:, pl.ds(start, WIDE)] = part[d * rows : (d + 1) * rows]


def whole(shape):
    return pl.BlockSpec(shape, lambda j: (0,) * len(shape))


def columns(shape):
    return pl.BlockSpec(shape, lambda j: (0, j))


def smem():
    return pl.BlockSpec(memory_space=pltpu.SMEM)


def params():
    return pltpu.CompilerParams(
        dimension_semantics=("arbitrary",), vmem_limit_bytes=VMEM_LIMIT
    )


def on_device(
    tokens,
    input_gain,
    gate_weight,
    inner_weight,
    state_weight,
    step_weight,
    step_bias,
    decay_exponent,
    conv_inner,
    conv_state,
    skip_gain,
    norm_gain,
    out_weight,
    passage_lengths,
):
    rows, width = tokens.shape
    heads = lax.axis_size("head")
    blocks = lax.axis_size("seq")
    heads_here = step_weight.shape[1]
    channels = heads_here * P_SIZE
    length = heads * rows
    passages = passage_lengths.shape[0]
    span = channels // 2
    steps = channels // CHUNK
    here = lax.axis_index("head")
    block = lax.axis_index("seq")
    place = jnp.stack([here, block * length]).astype(jnp.int32)

    def lanes3(a):
        a = jnp.concatenate([a] * 3, axis=-1)
        return jnp.pad(a, ((0, 0), (0, LANES - a.shape[1])))

    step_w = lanes3(step_weight)
    bias = lanes3(step_bias[None])
    rate = lanes3(decay_exponent.astype(F32)[None] * 2.0 ** (-21))
    skip = jnp.repeat(skip_gain, P_SIZE)[None]
    below, above, top, bottom, rim = map(far_memory, gather_tokens(tokens))

    def shape(dims, kind):
        return jax.ShapeDtypeStruct(dims, kind)

    half = rows // 2
    normed, sent, conv, scaled, cum, cum_rows, scores, maps, head_decay = pl.pallas_call(
        lambda *refs: block_kernel(*refs, heads_here=heads_here),
        grid=(steps,),
        in_specs=[
            smem(),
            whole((1, passages)),
            whole((passages, 1)),
            whole((rows, width)),
            whole((rows, width)),
            whole((rows, width)),
            whole((half, width)),
            whole((half + RIM, width)),
            whole((RIM, width)),
            whole((1, width)),
            whole((width, 2 * N)),
            whole((width, LANES)),
            whole((1, LANES)),
            whole((1, LANES)),
            whole((K, 2 * N)),
            columns((width, CHUNK)),
            columns((K, CHUNK)),
        ],
        out_specs=[
            whole((length, width)),
            whole((blocks, 8, span + LANES)),
            columns((length, CHUNK)),
            columns((length, CHUNK)),
            whole((length, LANES)),
            whole((LANES, length)),
            whole((length, length)),
            whole((length, N)),
            whole((length, LANES)),
        ],
        out_shape=[
            shape((length, width), BF16),
            shape((blocks, 8, span + LANES), BF16),
            shape((length, channels), BF16),
            shape((length, channels), BF16),
            shape((length, LANES), BF16),
            shape((LANES, length), F32),
            shape((length, length), F32),
            shape((length, N), BF16),
            shape((length, LANES), BF16),
        ],
        scratch_shapes=[
            pltpu.VMEM((length + RIM, width), BF16),
            pltpu.VMEM((K - 1, length, LANES), F32),
            pltpu.VMEM((length, LANES), BF16),
            pltpu.VMEM((length, LANES), BF16),
            pltpu.VMEM((N, length), BF16),
            pltpu.VMEM((N, channels), F32),
            pltpu.VMEM((RIM, LANES), F32),
        ],
        compiler_params=params(),
        name="block",
    )(
        place,
        passage_lengths[None],
        passage_lengths[:, None],
        tokens,
        below,
        above,
        top,
        bottom,
        rim,
        input_gain[None],
        state_weight,
        step_w,
        bias,
        rate,
        conv_state,
        inner_weight,
        conv_inner,
    )

    got = lax.all_to_all(sent, "seq", 0, 0, tiled=True)
    inside, gate = pl.pallas_call(
        lambda *refs: inside_kernel(*refs, heads_here=heads_here),
        grid=(steps,),
        in_specs=[
            whole((length, width)),
            columns((width, CHUNK)),
            columns((length, CHUNK)),
            columns((length, CHUNK)),
            whole((length, LANES)),
            whole((LANES, length)),
            whole((length, length)),
            columns((1, CHUNK)),
        ],
        out_specs=[columns((length, CHUNK)), columns((length, CHUNK))],
        out_shape=[shape((length, channels), F32), shape((length, channels), F32)],
        compiler_params=params(),
        name="inside",
    )(normed, gate_weight, scaled, conv, cum, cum_rows, scores, skip)

    back = pl.pallas_call(
        lambda *refs: scan_kernel(*refs, heads_here=heads_here),
        in_specs=[smem(), pl.BlockSpec(memory_space=pltpu.VMEM)],
        out_specs=pl.BlockSpec(memory_space=pltpu.VMEM),
        out_shape=shape((blocks, 8, span), BF16),
        compiler_params=pltpu.CompilerParams(vmem_limit_bytes=VMEM_LIMIT),
        name="scan",
    )(block.astype(jnp.int32)[None], got)
    states = far_memory(lax.all_to_all(back, "seq", 0, 0, tiled=True))

    out_width = out_weight.shape[1]
    parts = pl.pallas_call(
        lambda *refs: out_kernel(*refs, heads_here=heads_here),
        grid=(out_width // WIDE,),
        in_specs=[
            smem(),
            whole((blocks, 8, span)),
            whole((length, N)),
            whole((length, LANES)),
            whole((length, channels)),
            whole((length, channels)),
            whole((1, channels)),
            columns((channels, WIDE)),
        ],
        out_specs=[whole((rows, out_width + LANES))] * 4,
        out_shape=[shape((rows, out_width + LANES), BF16)] * 4,
        scratch_shapes=[
            pltpu.VMEM((N, channels), F32),
            pltpu.VMEM((length, channels), BF16),
            pltpu.VMEM((length, LANES), BF16),
        ],
        compiler_params=params(),
        name="out",
    )(place, states, maps, head_decay, inside, gate, norm_gain[None], out_weight)
    total = parts[0].astype(F32)
    for distance in range(1, heads):
        total = total + around(parts[distance], "head", distance).astype(F32)
    mean = jnp.sum(total[:, out_width : out_width + 3], axis=1, keepdims=True) / (H * P_SIZE)
    return (total[:, :out_width] * lax.rsqrt(mean + 1e-05)).astype(BF16)


def solution(mesh):
    in_specs = (
        P(("seq", "head"), None),
        P(),
        P(None, "head"),
        P(None, "head"),
        P(),
        P(None, "head"),
        P("head"),
        P("head"),
        P(None, "head"),
        P(),
        P("head"),
        P("head"),
        P("head", None),
        P(),
    )
    out_specs = P(("seq", "head"), None)
    return jax.shard_map(
        on_device, mesh=mesh, in_specs=in_specs, out_specs=out_specs, check_vma=False
    )
```

```python
import jax
import jax.numpy as jnp
from jax import lax
from jax.experimental import pallas as pl
from jax.experimental.pallas import tpu as pltpu
from jax.sharding import PartitionSpec as P

H = 80
P_SIZE = 64
N = 128
K = 4
RIM = 16
LANES = 128
CHUNK = 256
WIDE = 512
BLOCK_LIMIT = 16
INSIDE_LIMIT = 16
OUT_LIMIT = 16
SMALL_LIMIT = 8
F32 = jnp.float32
BF16 = jnp.bfloat16


def around(block, axis, distance):
    size = lax.axis_size(axis)
    return lax.ppermute(block, axis, [(i, (i + distance) % size) for i in range(size)])


def gather_tokens(tokens, inner_weight, state_weight):
    heads = lax.axis_size("head")
    blocks = lax.axis_size("seq")
    half = tokens.shape[0] // 2
    bottom = around(tokens[half:], "head", 2)
    below = around(tokens, "head", 1)
    above = around(tokens, "head", heads - 1)
    top = around(tokens[:half], "head", 2)
    (near,) = call(
        near_kernel,
        "near",
        [vmem()] * 2,
        [jax.ShapeDtypeStruct((16, LANES), tokens.dtype)],
        [],
        BLOCK_LIMIT,
    )(inner_weight, state_weight)
    (tail,) = call(
        tail_kernel,
        "tail",
        [vmem()] * 5,
        [jax.ShapeDtypeStruct((RIM, tokens.shape[1]), tokens.dtype)],
        [],
        SMALL_LIMIT,
    )(below, bottom, above, tokens, near)
    rim = lax.ppermute(tail, "seq", [(s, s + 1) for s in range(blocks - 1)])
    return below, above, top, bottom, rim


def split3(x):
    first = x.astype(BF16).astype(F32)
    rest = x - first
    second = rest.astype(BF16).astype(F32)
    return first, second, rest - second


def by_lane(x, count):
    lane = lax.broadcasted_iota(jnp.int32, x.shape, 1)
    first, second, third = split3(x)
    picked = jnp.where(lane < count, first, jnp.where(lane < 2 * count, second, third))
    return jnp.where(lane < 3 * count, picked, 0.0).astype(BF16)


def head_slot(shape, count):
    slot = lax.broadcasted_iota(jnp.int32, shape, 0)
    live = slot < 3 * count
    slot = slot - jnp.where(slot >= 2 * count, 2 * count, jnp.where(slot >= count, count, 0))
    return jnp.where(live, slot, -1)


def spread_matrix(first_head, width, count):
    shape = (LANES, width)
    head = first_head + lax.broadcasted_iota(jnp.int32, shape, 1) // P_SIZE
    return jnp.where(head_slot(shape, count) == head, 1.0, 0.0).astype(BF16)


def dot(a, b):
    return jnp.dot(a, b, preferred_element_type=F32)


def near_kernel(inner_w, state_w, near):
    near[...] = inner_w[0:16, 0:LANES] + state_w[0:16, 0:LANES]


def tail_kernel(below, bottom, above, own, near, tail):
    here = lax.axis_index("head")
    last = [x[x.shape[0] - RIM :, :] for x in (below, bottom, above, own)]
    low = jnp.where(here == 0, last[0], last[1])
    high = jnp.where(here == 2, last[2], last[3])
    tail[...] = jnp.where(here < 2, low, high)


def repeat_lanes(x):
    count = x.shape[1]
    lane = lax.broadcasted_iota(jnp.int32, (count, LANES), 1)
    slot = lax.broadcasted_iota(jnp.int32, (count, LANES), 0)
    hits = (lane == slot) | (lane == slot + count) | (lane == slot + 2 * count)
    copies = jnp.where(hits, 1.0, 0.0).astype(BF16)
    return sum(dot(part.astype(BF16), copies) for part in split3(x))


def block_kernel(
    lens_row,
    own,
    below,
    above,
    top,
    bottom,
    rim,
    gain,
    step_w,
    step_bias,
    rate,
    taps_state,
    taps_inner,
    state_w,
    inner_w,
    normed_out,
    sent,
    conv_out,
    scaled_out,
    cum_out,
    cum_rows,
    scores_out,
    maps_out,
    head_decay_out,
    normed,
    local,
    *,
    heads_here,
):
    rows = own.shape[0]
    length = normed.shape[0] - RIM
    here = lax.axis_index("head")
    first = lax.axis_index("seq") * length

    def norm(x):
        x = x.astype(F32)
        mean = jnp.mean(x * x, axis=-1, keepdims=True)
        return (x * lax.rsqrt(mean + 1e-05) * gain[...]).astype(BF16)

    def put(owner, offset, x):
        start = pl.multiple_of(RIM + owner * rows + offset, RIM)
        normed[pl.ds(start, x.shape[0]), :] = norm(x)

    half = rows // 2
    put(here, 0, own[...])
    put((here + 3) % 4, 0, below[...])
    put((here + 1) % 4, 0, above[...])
    far = (here + 2) % 4
    put(far, 0, top[...])
    put(far, half, bottom[...])
    normed[0:RIM, :] = norm(rim[...])
    normed_out[...] = normed[RIM:, :]

    passages = lens_row.shape[1]
    up = lax.broadcasted_iota(jnp.int32, (passages, passages), 0)
    across = lax.broadcasted_iota(jnp.int32, (passages, passages), 1)
    lens = jnp.broadcast_to(lens_row[...].astype(F32), (8, passages))
    whole = jnp.floor(lens * (1.0 / 128.0))
    before = jnp.where(up < across, 1.0, 0.0).astype(BF16)
    starts_row = 128.0 * dot(whole.astype(BF16), before)
    starts_row = (starts_row + dot((lens - 128.0 * whole).astype(BF16), before))[0:1]
    starts_col = jnp.sum(
        jnp.where(across < up, lens_row[...].astype(F32), 0.0), axis=1, keepdims=True
    )
    base = first.astype(F32)
    pos = lax.broadcasted_iota(jnp.int32, (length + RIM, passages), 0).astype(F32)
    ids_pad = jnp.sum(
        jnp.where(pos + (base - RIM) >= starts_row, 1.0, 0.0), axis=1, keepdims=True
    )
    pos = lax.broadcasted_iota(jnp.int32, (passages, length), 1).astype(F32)
    ids_row = jnp.sum(jnp.where(pos + base >= starts_col, 1.0, 0.0), axis=0, keepdims=True)
    ids_wide = jnp.broadcast_to(ids_pad, (length + RIM, LANES))
    ids = ids_wide[RIM:]
    agree = [
        jnp.where(pltpu.roll(ids_wide, lag, 0)[RIM:] == ids, 1.0, 0.0) for lag in range(1, K)
    ]

    def conv(raw, taps):
        acc = taps[0:1] * raw[RIM:]
        for lag in range(1, K):
            moved = pltpu.roll(raw, lag, 0)[RIM:]
            same = jnp.concatenate([agree[lag - 1]] * (raw.shape[1] // LANES), axis=1)
            acc = acc + taps[lag : lag + 1] * moved * same
        return (acc * jax.nn.sigmoid(acc)).astype(BF16)

    x = lax.dot_general(
        normed[RIM:, :], step_w[...], (((1,), (1,)), ((), ())), preferred_element_type=F32
    )
    x = repeat_lanes(x + step_bias[...])
    rates = jnp.broadcast_to(rate[...].astype(F32) * 2.0 ** (-21), (8, rate.shape[1]))
    raw = dot(normed[...], state_w[...]).astype(BF16).astype(F32)
    maps = conv(raw, taps_state[...])
    maps_in = maps[:, :N]
    maps_out[...] = maps[:, N:]
    maps_in_t = maps_in.astype(F32).T.astype(BF16)
    t = lax.broadcasted_iota(jnp.int32, (length, length), 0)
    s = lax.broadcasted_iota(jnp.int32, (length, length), 1)
    ids_two = jnp.concatenate([ids] * (length // LANES), axis=1)
    mask = (ids_two == ids_row) & (t >= s)
    scores_out[...] = jnp.where(mask, dot(maps[:, N:], maps_in_t), 0.0)

    step = jnp.maximum(x, 0.0) + jnp.log1p(jnp.exp(-jnp.abs(x)))
    log_decay = -step * repeat_lanes(rates)[0:1]
    ones = jnp.where(t >= s, 1.0, 0.0).astype(BF16)
    cum = sum(dot(ones, part.astype(BF16)) for part in split3(log_decay))
    last = cum[length - 1 :, :]
    ids_last = ids[length - 1 :, :]
    prior = ids_wide[RIM - 1 : RIM, :]
    step3 = by_lane(step, heads_here)
    tail = jnp.exp(jnp.minimum(last - cum, 0.0)) * jnp.where(ids == ids_last, 1.0, 0.0)
    tail3 = by_lane(tail, heads_here)
    keep = jnp.exp(cum) * jnp.where(ids == prior, 1.0, 0.0)
    keep3 = by_lane(keep, heads_here)
    head_decay_out[...] = keep3
    cum_out[...] = by_lane(cum, heads_here)
    cum_rows[...] = cum.T

    for c in range(local.shape[1] // CHUNK):
        cols = slice(c * CHUNK, (c + 1) * CHUNK)
        raw = dot(normed[...], inner_w[:, cols]).astype(BF16).astype(F32)
        mixed = conv(raw, taps_inner[:, cols])
        conv_out[:, cols] = mixed
        spread = spread_matrix(c * (CHUNK // P_SIZE), CHUNK, heads_here)
        scaled = (mixed.astype(F32) * dot(step3, spread)).astype(BF16)
        scaled_out[:, cols] = scaled
        tail_in = (dot(tail3, spread) * scaled.astype(F32)).astype(BF16)
        local[:, cols] = dot(maps_in_t, tail_in)

    span = local.shape[1] // 2
    decay = jnp.broadcast_to(keep3[length - RIM :].astype(F32)[RIM - 1 :], (8, LANES))
    for piece in range(sent.shape[0]):
        group, side = piece // 2, piece % 2
        part = local[8 * group : 8 * group + 8, side * span : (side + 1) * span]
        sent[piece, :, 0:span] = part.astype(BF16)
        sent[piece, :, span:] = decay.astype(BF16)


def inside_kernel(
    normed,
    scaled,
    conv,
    cum,
    cum_rows,
    scores,
    skip,
    gate_w,
    inside,
    gate,
    *,
    heads_here,
):
    length = scaled.shape[0]
    half = length // 2
    per = CHUNK // P_SIZE
    lane = lax.broadcasted_iota(jnp.int32, (length, CHUNK), 1) // P_SIZE
    slots = head_slot((LANES, length), heads_here)
    skip3 = by_lane(repeat_lanes(jnp.broadcast_to(skip[...], (8, heads_here))), heads_here)
    for c in range(scaled.shape[1] // CHUNK):
        cols = slice(c * CHUNK, (c + 1) * CHUNK)
        x = scaled[:, cols]
        tops, bottoms, top_x, all_x = [], [], [], []
        for i in range(per):
            head = c * per + i
            pick = jnp.where(slots == head, 1.0, 0.0).astype(BF16)
            cum_t = dot(cum[...], pick)
            cum_s = cum_rows[head : head + 1, :]
            own = jnp.where(lane == i, x, jnp.zeros_like(x))
            upper = jnp.exp(jnp.minimum(cum_t[:half, :half] - cum_s[:, :half], 0.0))
            lower = jnp.exp(jnp.minimum(cum_t[half:] - cum_s, 0.0))
            tops.append((upper * scores[0:half, 0:half]).astype(BF16))
            bottoms.append((lower * scores[half:, :]).astype(BF16))
            top_x.append(own[:half])
            all_x.append(own)
        spread = spread_matrix(c * per, CHUNK, heads_here)
        skips = dot(skip3, spread)[0:1]
        upper = dot(jnp.concatenate(tops, axis=1), jnp.concatenate(top_x, axis=0))
        lower = dot(jnp.concatenate(bottoms, axis=1), jnp.concatenate(all_x, axis=0))
        inside[:, cols] = jnp.concatenate([upper, lower], axis=0) + (
            skips * conv[:, cols].astype(F32)
        )
        vals = dot(normed[...], gate_w[:, cols]).astype(BF16).astype(F32)
        gate[:, cols] = vals * jax.nn.sigmoid(vals)


def scan_kernel(got, back, *, heads_here):
    blocks, depth, width = got.shape
    span = width - LANES
    side = lax.axis_index("seq") % 2
    spread = spread_matrix(side * (span // P_SIZE), span, heads_here)
    parts = got[:, :, span:].astype(F32).reshape(blocks * depth, LANES).astype(BF16)
    decay = dot(parts, spread)
    state = jnp.zeros((depth, span), F32)
    for b in range(blocks):
        back[b] = state.astype(BF16)
        if b < blocks - 1:
            state = decay[b * depth : (b + 1) * depth] * state + got[b, :, 0:span].astype(F32)


def out_kernel(
    got,
    maps,
    head_decay,
    inside,
    gate,
    norm_gain,
    out_w,
    out0,
    out1,
    out2,
    out2b,
    out3,
    states,
    x,
    sums,
    *,
    heads_here,
):
    length = inside.shape[0]
    rows = length // 4
    half = rows // 2
    here = lax.axis_index("head")
    span = got.shape[2]
    for piece in range(got.shape[0]):
        group, side = piece // 2, piece % 2
        states[8 * group : 8 * group + 8, side * span : (side + 1) * span] = got[piece].astype(
            F32
        )
    total = jnp.zeros((length, 1), F32)
    for c in range(inside.shape[1] // CHUNK):
        cols = slice(c * CHUNK, (c + 1) * CHUNK)
        spread = spread_matrix(c * (CHUNK // P_SIZE), CHUNK, heads_here)
        carried = dot(maps[...], states[:, cols].astype(BF16)) * dot(head_decay[...], spread)
        gated = (inside[:, cols] + carried) * gate[:, cols]
        total = total + jnp.sum(gated * gated, axis=1, keepdims=True)
        ready = (gated * norm_gain[:, cols]).astype(BF16)
        for b in range(4):
            start = pl.multiple_of(((b + 4 - here) % 4) * rows, rows)
            x[pl.ds(start, rows), cols] = ready[b * rows : (b + 1) * rows]
    packed = by_lane(jnp.broadcast_to(total, (length, LANES)), 1)
    for b in range(4):
        start = pl.multiple_of(((b + 4 - here) % 4) * rows, rows)
        sums[pl.ds(start, rows), :] = packed[b * rows : (b + 1) * rows]

    def put(cols, part):
        out0[:, cols] = part[0:rows]
        out1[:, cols] = part[rows : 2 * rows]
        out2[:, cols] = part[2 * rows : 2 * rows + half]
        out2b[:, cols] = part[2 * rows + half : 3 * rows]
        out3[:, cols] = part[3 * rows :]

    width = out_w.shape[1]
    for c in range(width // WIDE):
        cols = slice(c * WIDE, (c + 1) * WIDE)
        put(cols, dot(x[...], out_w[:, cols]).astype(BF16))
    put(slice(width, width + LANES), sums[...])


def close_kernel(own, one, two, two_b, three, mixed):
    width = mixed.shape[1]
    half = two.shape[0]
    for i, far in enumerate((two, two_b)):
        rows = slice(i * half, (i + 1) * half)
        total = own[rows, :].astype(F32) + one[rows, :].astype(F32)
        total = total + far[...].astype(F32) + three[rows, :].astype(F32)
        mean = jnp.sum(total[:, width:], axis=1, keepdims=True) / (H * P_SIZE)
        mixed[rows, :] = (total[:, :width] * lax.rsqrt(mean + 1e-05)).astype(BF16)


def vmem():
    return pl.BlockSpec(memory_space=pltpu.VMEM)


def call(kernel, name, in_specs, out_shape, scratch_shapes, limit):
    return pl.pallas_call(
        kernel,
        in_specs=in_specs,
        out_specs=[vmem()] * len(out_shape),
        out_shape=out_shape,
        scratch_shapes=scratch_shapes,
        compiler_params=pltpu.CompilerParams(vmem_limit_bytes=limit << 20),
        name=name,
    )


def on_device(
    tokens,
    input_gain,
    gate_weight,
    inner_weight,
    state_weight,
    step_weight,
    step_bias,
    decay_exponent,
    conv_inner,
    conv_state,
    skip_gain,
    norm_gain,
    out_weight,
    passage_lengths,
):
    rows, width = tokens.shape
    heads = lax.axis_size("head")
    blocks = lax.axis_size("seq")
    heads_here = step_weight.shape[1]
    channels = heads_here * P_SIZE
    length = heads * rows
    passages = passage_lengths.shape[0]
    span = channels // 2
    below, above, top, bottom, rim = gather_tokens(tokens, inner_weight, state_weight)

    def shape(dims, kind):
        return jax.ShapeDtypeStruct(dims, kind)

    normed, sent, conv, scaled, cum, cum_rows, scores, maps, head_decay = call(
        lambda *refs: block_kernel(*refs, heads_here=heads_here),
        "block",
        [vmem()] * 15,
        [
            shape((length, width), BF16),
            shape((blocks, 8, span + LANES), BF16),
            shape((length, channels), BF16),
            shape((length, channels), BF16),
            shape((length, LANES), BF16),
            shape((LANES, length), F32),
            shape((length, length), F32),
            shape((length, N), BF16),
            shape((length, LANES), BF16),
        ],
        [
            pltpu.VMEM((length + RIM, width), BF16),
            pltpu.VMEM((N, channels), F32),
        ],
        BLOCK_LIMIT,
    )(
        passage_lengths[None],
        tokens,
        below,
        above,
        top,
        bottom,
        rim,
        input_gain[None],
        step_weight.T,
        step_bias[None],
        decay_exponent[None],
        conv_state,
        conv_inner,
        state_weight,
        inner_weight,
    )

    inside, gate = call(
        lambda *refs: inside_kernel(*refs, heads_here=heads_here),
        "inside",
        [vmem()] * 8,
        [shape((length, channels), F32), shape((length, channels), F32)],
        [],
        INSIDE_LIMIT,
    )(normed, scaled, conv, cum, cum_rows, scores, skip_gain[None], gate_weight)
    sent, inside, gate, out_gain = lax.optimization_barrier(
        (sent, inside, gate, norm_gain[None])
    )
    got = lax.all_to_all(sent, "seq", 0, 0, tiled=True)

    (back,) = call(
        lambda *refs: scan_kernel(*refs, heads_here=heads_here),
        "scan",
        [vmem()],
        [shape((blocks, 8, span), BF16)],
        [],
        SMALL_LIMIT,
    )(got)
    states = lax.all_to_all(back, "seq", 0, 0, tiled=True)

    out_width = out_weight.shape[1]
    packed = out_width + LANES
    own, one, two, two_b, three = call(
        lambda *refs: out_kernel(*refs, heads_here=heads_here),
        "out",
        [vmem()] * 7,
        [shape((n, packed), BF16) for n in (rows, rows, rows // 2, rows // 2, rows)],
        [
            pltpu.VMEM((N, channels), F32),
            pltpu.VMEM((length, channels), BF16),
            pltpu.VMEM((length, LANES), BF16),
        ],
        OUT_LIMIT,
    )(states, maps, head_decay, inside, gate, out_gain, out_weight)
    (mixed,) = call(
        close_kernel,
        "close",
        [vmem()] * 5,
        [shape((rows, out_width), BF16)],
        [],
        SMALL_LIMIT,
    )(
        own,
        around(one, "head", 1),
        around(two, "head", 2),
        around(two_b, "head", 2),
        around(three, "head", 3),
    )
    return mixed


def solution(mesh):
    in_specs = (
        P(("seq", "head"), None),
        P(),
        P(None, "head"),
        P(None, "head"),
        P(),
        P(None, "head"),
        P("head"),
        P("head"),
        P(None, "head"),
        P(),
        P("head"),
        P("head"),
        P("head", None),
        P(),
    )
    out_specs = P(("seq", "head"), None)
    return jax.shard_map(
        on_device, mesh=mesh, in_specs=in_specs, out_specs=out_specs, check_vma=False
    )
```

```python
import jax
import jax.numpy as jnp
from jax import lax
from jax.experimental import pallas as pl
from jax.experimental.pallas import tpu as pltpu
from jax.sharding import PartitionSpec as P

H = 80
P_SIZE = 64
N = 128
K = 4
RIM = 16
LANES = 128
CHUNK = 256
WIDE = 512
BLOCK_LIMIT = 16
INSIDE_LIMIT = 16
OUT_LIMIT = 16
SMALL_LIMIT = 8
F32 = jnp.float32
BF16 = jnp.bfloat16


def around(block, axis, distance):
    size = lax.axis_size(axis)
    return lax.ppermute(block, axis, [(i, (i + distance) % size) for i in range(size)])


def gather_tokens(tokens, inner_weight, state_weight):
    heads = lax.axis_size("head")
    blocks = lax.axis_size("seq")
    rows, width = tokens.shape
    half = rows // 2
    below = around(tokens, "head", 1)
    above = around(tokens, "head", heads - 1)
    bottom = around(tokens[half:], "head", 2)
    top = around(tokens[:half], "head", 2)
    last = heads - 1
    far = [(s * heads + last, (s + 1) * heads + 1) for s in range(blocks - 1)]
    rim_far = lax.ppermute(tokens[rows - RIM :], ("seq", "head"), far)
    (near,) = call(
        near_kernel,
        "near",
        [vmem()] * 2,
        [jax.ShapeDtypeStruct((RIM, LANES), tokens.dtype)],
        [],
        BLOCK_LIMIT,
    )(inner_weight, state_weight)
    (tail,) = call(
        tail_kernel,
        "tail",
        [vmem()] * 4,
        [jax.ShapeDtypeStruct((RIM, width), tokens.dtype)],
        [],
        SMALL_LIMIT,
    )(below, above, tokens, near)
    route = [
        (s * heads + h, (s + 1) * heads + h)
        for s in range(blocks - 1)
        for h in range(heads)
        if h != 1
    ]
    return below, above, top, bottom, lax.ppermute(tail, ("seq", "head"), route), rim_far


def split3(x):
    first = x.astype(BF16).astype(F32)
    rest = x - first
    second = rest.astype(BF16).astype(F32)
    return first, second, rest - second


def by_lane(x, count):
    lane = lax.broadcasted_iota(jnp.int32, x.shape, 1)
    first, second, third = split3(x)
    picked = jnp.where(lane < count, first, jnp.where(lane < 2 * count, second, third))
    return jnp.where(lane < 3 * count, picked, 0.0).astype(BF16)


def head_slot(shape, count):
    slot = lax.broadcasted_iota(jnp.int32, shape, 0)
    live = slot < 3 * count
    slot = slot - jnp.where(slot >= 2 * count, 2 * count, jnp.where(slot >= count, count, 0))
    return jnp.where(live, slot, -1)


def spread_matrix(first_head, width, count):
    shape = (LANES, width)
    head = first_head + lax.broadcasted_iota(jnp.int32, shape, 1) // P_SIZE
    return jnp.where(head_slot(shape, count) == head, 1.0, 0.0).astype(BF16)


def dot(a, b):
    return jnp.dot(a, b, preferred_element_type=F32)


def near_kernel(inner_w, state_w, near):
    near[...] = inner_w[0:RIM, 0:LANES] + state_w[0:RIM, 0:LANES]


def tail_kernel(below, above, own, near, tail):
    here = lax.axis_index("head")
    last = [x[x.shape[0] - RIM :, :] for x in (below, above, own)]
    tail[...] = jnp.where(here == 0, last[0], jnp.where(here == 2, last[1], last[2]))


def repeat_lanes(x):
    count = x.shape[1]
    lane = lax.broadcasted_iota(jnp.int32, (count, LANES), 1)
    slot = lax.broadcasted_iota(jnp.int32, (count, LANES), 0)
    hits = (lane == slot) | (lane == slot + count) | (lane == slot + 2 * count)
    copies = jnp.where(hits, 1.0, 0.0).astype(BF16)
    return sum(dot(part.astype(BF16), copies) for part in split3(x))


def block_kernel(
    lens_row,
    own,
    below,
    above,
    top,
    bottom,
    rim,
    rim_far,
    gain,
    step_w,
    step_bias,
    rate,
    taps_state,
    taps_inner,
    state_w,
    inner_w,
    normed_out,
    sent,
    conv_out,
    scaled_out,
    cum_out,
    cum_rows,
    scores_out,
    maps_out,
    head_decay_out,
    normed,
    local,
    *,
    heads_here,
):
    rows = own.shape[0]
    length = normed.shape[0] - RIM
    here = lax.axis_index("head")
    first = lax.axis_index("seq") * length

    def norm(x):
        x = x.astype(F32)
        mean = jnp.mean(x * x, axis=-1, keepdims=True)
        return (x * lax.rsqrt(mean + 1e-05) * gain[...]).astype(BF16)

    def put(owner, offset, x):
        start = pl.multiple_of(RIM + owner * rows + offset, RIM)
        normed[pl.ds(start, x.shape[0]), :] = norm(x)

    half = rows // 2
    put(here, 0, own[...])
    put((here + 3) % 4, 0, below[...])
    put((here + 1) % 4, 0, above[...])
    far = (here + 2) % 4
    put(far, 0, top[...])
    put(far, half, bottom[...])
    normed[0:RIM, :] = norm(rim[...] + rim_far[...])
    normed_out[...] = normed[RIM:, :]

    passages = lens_row.shape[1]
    up = lax.broadcasted_iota(jnp.int32, (passages, passages), 0)
    across = lax.broadcasted_iota(jnp.int32, (passages, passages), 1)
    lens = jnp.broadcast_to(lens_row[...].astype(F32), (8, passages))
    whole = jnp.floor(lens * (1.0 / 128.0))
    before = jnp.where(up < across, 1.0, 0.0).astype(BF16)
    starts_row = 128.0 * dot(whole.astype(BF16), before)
    starts_row = (starts_row + dot((lens - 128.0 * whole).astype(BF16), before))[0:1]
    starts_col = jnp.sum(
        jnp.where(across < up, lens_row[...].astype(F32), 0.0), axis=1, keepdims=True
    )
    base = first.astype(F32)
    pos = lax.broadcasted_iota(jnp.int32, (length + RIM, passages), 0).astype(F32)
    ids_pad = jnp.sum(
        jnp.where(pos + (base - RIM) >= starts_row, 1.0, 0.0), axis=1, keepdims=True
    )
    pos = lax.broadcasted_iota(jnp.int32, (passages, length), 1).astype(F32)
    ids_row = jnp.sum(jnp.where(pos + base >= starts_col, 1.0, 0.0), axis=0, keepdims=True)
    ids_wide = jnp.broadcast_to(ids_pad, (length + RIM, LANES))
    ids = ids_wide[RIM:]
    agree = [
        jnp.where(pltpu.roll(ids_wide, lag, 0)[RIM:] == ids, 1.0, 0.0) for lag in range(1, K)
    ]

    def conv(raw, taps):
        acc = taps[0:1] * raw[RIM:]
        for lag in range(1, K):
            moved = pltpu.roll(raw, lag, 0)[RIM:]
            same = jnp.concatenate([agree[lag - 1]] * (raw.shape[1] // LANES), axis=1)
            acc = acc + taps[lag : lag + 1] * moved * same
        return (acc * jax.nn.sigmoid(acc)).astype(BF16)

    x = lax.dot_general(
        normed[RIM:, :], step_w[...], (((1,), (1,)), ((), ())), preferred_element_type=F32
    )
    x = repeat_lanes(x + step_bias[...])
    rates = jnp.broadcast_to(rate[...].astype(F32) * 2.0 ** (-21), (8, rate.shape[1]))
    raw = dot(normed[...], state_w[...]).astype(BF16).astype(F32)
    maps = conv(raw, taps_state[...])
    maps_in = maps[:, :N]
    maps_out[...] = maps[:, N:]
    maps_in_t = maps_in.astype(F32).T.astype(BF16)
    t = lax.broadcasted_iota(jnp.int32, (length, length), 0)
    s = lax.broadcasted_iota(jnp.int32, (length, length), 1)
    ids_two = jnp.concatenate([ids] * (length // LANES), axis=1)
    mask = (ids_two == ids_row) & (t >= s)
    scores_out[...] = jnp.where(mask, dot(maps[:, N:], maps_in_t), 0.0)

    step = jnp.maximum(x, 0.0) + jnp.log1p(jnp.exp(-jnp.abs(x)))
    log_decay = -step * repeat_lanes(rates)[0:1]
    ones = jnp.where(t >= s, 1.0, 0.0).astype(BF16)
    cum = sum(dot(ones, part.astype(BF16)) for part in split3(log_decay))
    last = cum[length - 1 :, :]
    ids_last = ids[length - 1 :, :]
    prior = ids_wide[RIM - 1 : RIM, :]
    step3 = by_lane(step, heads_here)
    tail = jnp.exp(jnp.minimum(last - cum, 0.0)) * jnp.where(ids == ids_last, 1.0, 0.0)
    tail3 = by_lane(tail, heads_here)
    keep = jnp.exp(cum) * jnp.where(ids == prior, 1.0, 0.0)
    keep3 = by_lane(keep, heads_here)
    head_decay_out[...] = keep3
    cum_out[...] = by_lane(cum, heads_here)
    cum_rows[...] = cum.T

    for c in range(local.shape[1] // CHUNK):
        cols = slice(c * CHUNK, (c + 1) * CHUNK)
        raw = dot(normed[...], inner_w[:, cols]).astype(BF16).astype(F32)
        mixed = conv(raw, taps_inner[:, cols])
        conv_out[:, cols] = mixed
        spread = spread_matrix(c * (CHUNK // P_SIZE), CHUNK, heads_here)
        scaled = (mixed.astype(F32) * dot(step3, spread)).astype(BF16)
        scaled_out[:, cols] = scaled
        tail_in = (dot(tail3, spread) * scaled.astype(F32)).astype(BF16)
        local[:, cols] = dot(maps_in_t, tail_in)

    span = local.shape[1] // 2
    decay = jnp.broadcast_to(keep3[length - RIM :].astype(F32)[RIM - 1 :], (8, LANES))
    for piece in range(sent.shape[0]):
        group, side = piece // 2, piece % 2
        part = local[8 * group : 8 * group + 8, side * span : (side + 1) * span]
        sent[piece, :, 0:span] = part.astype(BF16)
        sent[piece, :, span:] = decay.astype(BF16)


def inside_kernel(
    normed,
    scaled,
    conv,
    cum,
    cum_rows,
    scores,
    skip,
    gate_w,
    inside,
    gate,
    *,
    heads_here,
):
    length = scaled.shape[0]
    half = length // 2
    per = CHUNK // P_SIZE
    lane = lax.broadcasted_iota(jnp.int32, (length, CHUNK), 1) // P_SIZE
    slots = head_slot((LANES, length), heads_here)
    skip3 = by_lane(repeat_lanes(jnp.broadcast_to(skip[...], (8, heads_here))), heads_here)
    for c in range(scaled.shape[1] // CHUNK):
        cols = slice(c * CHUNK, (c + 1) * CHUNK)
        x = scaled[:, cols]
        tops, bottoms, top_x, all_x = [], [], [], []
        for i in range(per):
            head = c * per + i
            pick = jnp.where(slots == head, 1.0, 0.0).astype(BF16)
            cum_t = dot(cum[...], pick)
            cum_s = cum_rows[head : head + 1, :]
            own = jnp.where(lane == i, x, jnp.zeros_like(x))
            upper = jnp.exp(jnp.minimum(cum_t[:half, :half] - cum_s[:, :half], 0.0))
            lower = jnp.exp(jnp.minimum(cum_t[half:] - cum_s, 0.0))
            tops.append((upper * scores[0:half, 0:half]).astype(BF16))
            bottoms.append((lower * scores[half:, :]).astype(BF16))
            top_x.append(own[:half])
            all_x.append(own)
        spread = spread_matrix(c * per, CHUNK, heads_here)
        skips = dot(skip3, spread)[0:1]
        upper = dot(jnp.concatenate(tops, axis=1), jnp.concatenate(top_x, axis=0))
        lower = dot(jnp.concatenate(bottoms, axis=1), jnp.concatenate(all_x, axis=0))
        inside[:, cols] = jnp.concatenate([upper, lower], axis=0) + (
            skips * conv[:, cols].astype(F32)
        )
        vals = dot(normed[...], gate_w[:, cols]).astype(BF16).astype(F32)
        gate[:, cols] = vals * jax.nn.sigmoid(vals)


def scan_kernel(got, back, *, heads_here):
    blocks, depth, width = got.shape
    span = width - LANES
    side = lax.axis_index("seq") % 2
    spread = spread_matrix(side * (span // P_SIZE), span, heads_here)
    parts = got[:, :, span:].astype(F32).reshape(blocks * depth, LANES).astype(BF16)
    decay = dot(parts, spread)
    state = jnp.zeros((depth, span), F32)
    for b in range(blocks):
        back[b] = state.astype(BF16)
        if b < blocks - 1:
            state = decay[b * depth : (b + 1) * depth] * state + got[b, :, 0:span].astype(F32)


def out_kernel(
    got,
    maps,
    head_decay,
    inside,
    gate,
    norm_gain,
    out_w,
    out0,
    out1,
    out2,
    out2b,
    out3,
    states,
    x,
    sums,
    *,
    heads_here,
):
    length = inside.shape[0]
    rows = length // 4
    half = rows // 2
    here = lax.axis_index("head")
    span = got.shape[2]
    for piece in range(got.shape[0]):
        group, side = piece // 2, piece % 2
        states[8 * group : 8 * group + 8, side * span : (side + 1) * span] = got[piece].astype(
            F32
        )
    total = jnp.zeros((length, 1), F32)
    for c in range(inside.shape[1] // CHUNK):
        cols = slice(c * CHUNK, (c + 1) * CHUNK)
        spread = spread_matrix(c * (CHUNK // P_SIZE), CHUNK, heads_here)
        carried = dot(maps[...], states[:, cols].astype(BF16)) * dot(head_decay[...], spread)
        gated = (inside[:, cols] + carried) * gate[:, cols]
        total = total + jnp.sum(gated * gated, axis=1, keepdims=True)
        ready = (gated * norm_gain[:, cols]).astype(BF16)
        for b in range(4):
            start = pl.multiple_of(((b + 4 - here) % 4) * rows, rows)
            x[pl.ds(start, rows), cols] = ready[b * rows : (b + 1) * rows]
    packed = by_lane(jnp.broadcast_to(total, (length, LANES)), 1)
    for b in range(4):
        start = pl.multiple_of(((b + 4 - here) % 4) * rows, rows)
        sums[pl.ds(start, rows), :] = packed[b * rows : (b + 1) * rows]

    def put(cols, part):
        out0[:, cols] = part[0:rows]
        out1[:, cols] = part[rows : 2 * rows]
        out2[:, cols] = part[2 * rows : 2 * rows + half]
        out2b[:, cols] = part[2 * rows + half : 3 * rows]
        out3[:, cols] = part[3 * rows :]

    width = out_w.shape[1]
    for c in range(width // WIDE):
        cols = slice(c * WIDE, (c + 1) * WIDE)
        put(cols, dot(x[...], out_w[:, cols]).astype(BF16))
    put(slice(width, width + LANES), sums[...])


def close_kernel(own, one, two, two_b, three, mixed):
    width = mixed.shape[1]
    half = two.shape[0]
    for i, far in enumerate((two, two_b)):
        rows = slice(i * half, (i + 1) * half)
        total = own[rows, :].astype(F32) + one[rows, :].astype(F32)
        total = total + far[...].astype(F32) + three[rows, :].astype(F32)
        mean = jnp.sum(total[:, width:], axis=1, keepdims=True) / (H * P_SIZE)
        mixed[rows, :] = (total[:, :width] * lax.rsqrt(mean + 1e-05)).astype(BF16)


def vmem():
    return pl.BlockSpec(memory_space=pltpu.VMEM)


def call(kernel, name, in_specs, out_shape, scratch_shapes, limit):
    return pl.pallas_call(
        kernel,
        in_specs=in_specs,
        out_specs=[vmem()] * len(out_shape),
        out_shape=out_shape,
        scratch_shapes=scratch_shapes,
        compiler_params=pltpu.CompilerParams(vmem_limit_bytes=limit << 20),
        name=name,
    )


def on_device(
    tokens,
    input_gain,
    gate_weight,
    inner_weight,
    state_weight,
    step_weight,
    step_bias,
    decay_exponent,
    conv_inner,
    conv_state,
    skip_gain,
    norm_gain,
    out_weight,
    passage_lengths,
):
    rows, width = tokens.shape
    heads = lax.axis_size("head")
    blocks = lax.axis_size("seq")
    heads_here = step_weight.shape[1]
    channels = heads_here * P_SIZE
    length = heads * rows
    passages = passage_lengths.shape[0]
    span = channels // 2
    below, above, top, bottom, rim, rim_far = gather_tokens(tokens, inner_weight, state_weight)

    def shape(dims, kind):
        return jax.ShapeDtypeStruct(dims, kind)

    normed, sent, conv, scaled, cum, cum_rows, scores, maps, head_decay = call(
        lambda *refs: block_kernel(*refs, heads_here=heads_here),
        "block",
        [vmem()] * 16,
        [
            shape((length, width), BF16),
            shape((blocks, 8, span + LANES), BF16),
            shape((length, channels), BF16),
            shape((length, channels), BF16),
            shape((length, LANES), BF16),
            shape((LANES, length), F32),
            shape((length, length), F32),
            shape((length, N), BF16),
            shape((length, LANES), BF16),
        ],
        [
            pltpu.VMEM((length + RIM, width), BF16),
            pltpu.VMEM((N, channels), F32),
        ],
        BLOCK_LIMIT,
    )(
        passage_lengths[None],
        tokens,
        below,
        above,
        top,
        bottom,
        rim,
        rim_far,
        input_gain[None],
        step_weight.T,
        step_bias[None],
        decay_exponent[None],
        conv_state,
        conv_inner,
        state_weight,
        inner_weight,
    )

    inside, gate = call(
        lambda *refs: inside_kernel(*refs, heads_here=heads_here),
        "inside",
        [vmem()] * 8,
        [shape((length, channels), F32), shape((length, channels), F32)],
        [],
        INSIDE_LIMIT,
    )(normed, scaled, conv, cum, cum_rows, scores, skip_gain[None], gate_weight)
    sent, inside, gate, out_gain = lax.optimization_barrier(
        (sent, inside, gate, norm_gain[None])
    )
    got = lax.all_to_all(sent, "seq", 0, 0, tiled=True)

    (back,) = call(
        lambda *refs: scan_kernel(*refs, heads_here=heads_here),
        "scan",
        [vmem()],
        [shape((blocks, 8, span), BF16)],
        [],
        SMALL_LIMIT,
    )(got)
    states = lax.all_to_all(back, "seq", 0, 0, tiled=True)

    out_width = out_weight.shape[1]
    packed = out_width + LANES
    own, one, two, two_b, three = call(
        lambda *refs: out_kernel(*refs, heads_here=heads_here),
        "out",
        [vmem()] * 7,
        [shape((n, packed), BF16) for n in (rows, rows, rows // 2, rows // 2, rows)],
        [
            pltpu.VMEM((N, channels), F32),
            pltpu.VMEM((length, channels), BF16),
            pltpu.VMEM((length, LANES), BF16),
        ],
        OUT_LIMIT,
    )(states, maps, head_decay, inside, gate, out_gain, out_weight)
    (mixed,) = call(
        close_kernel,
        "close",
        [vmem()] * 5,
        [shape((rows, out_width), BF16)],
        [],
        SMALL_LIMIT,
    )(
        own,
        around(one, "head", 1),
        around(two, "head", 2),
        around(two_b, "head", 2),
        around(three, "head", 3),
    )
    return mixed


def solution(mesh):
    in_specs = (
        P(("seq", "head"), None),
        P(),
        P(None, "head"),
        P(None, "head"),
        P(),
        P(None, "head"),
        P("head"),
        P("head"),
        P(None, "head"),
        P(),
        P("head"),
        P("head"),
        P("head", None),
        P(),
    )
    out_specs = P(("seq", "head"), None)
    return jax.shard_map(
        on_device, mesh=mesh, in_specs=in_specs, out_specs=out_specs, check_vma=False
    )
```

```python
import jax
import jax.numpy as jnp
from jax import lax
from jax.experimental import pallas as pl
from jax.experimental.pallas import tpu as pltpu
from jax.sharding import PartitionSpec as P

H = 80
P_SIZE = 64
N = 128
K = 4
RIM = 16
LANES = 128
CHUNK = 256
WIDE = 512
BLOCK_LIMIT = 16
INSIDE_LIMIT = 16
OUT_LIMIT = 16
SMALL_LIMIT = 8
F32 = jnp.float32
BF16 = jnp.bfloat16


def around(block, axis, distance):
    size = lax.axis_size(axis)
    return lax.ppermute(block, axis, [(i, (i + distance) % size) for i in range(size)])


def gather_tokens(tokens, inner_weight, state_weight):
    heads = lax.axis_size("head")
    blocks = lax.axis_size("seq")
    rows, width = tokens.shape
    half = rows // 2
    below = around(tokens, "head", 1)
    above = around(tokens, "head", heads - 1)
    bottom = around(tokens[half:], "head", 2)
    top = around(tokens[:half], "head", 2)
    last = heads - 1
    far = [(s * heads + last, (s + 1) * heads + 1) for s in range(blocks - 1)]
    rim_far = lax.ppermute(tokens[rows - RIM :], ("seq", "head"), far)
    (near,) = call(
        near_kernel,
        "near",
        [vmem()] * 2,
        [jax.ShapeDtypeStruct((RIM, LANES), tokens.dtype)],
        [],
        BLOCK_LIMIT,
    )(inner_weight, state_weight)
    (tail,) = call(
        tail_kernel,
        "tail",
        [vmem()] * 4,
        [jax.ShapeDtypeStruct((RIM, width), tokens.dtype)],
        [],
        SMALL_LIMIT,
    )(below, above, tokens, near)
    route = [
        (s * heads + h, (s + 1) * heads + h)
        for s in range(blocks - 1)
        for h in range(heads)
        if h != 1
    ]
    return below, above, top, bottom, lax.ppermute(tail, ("seq", "head"), route), rim_far


def split3(x):
    first = x.astype(BF16).astype(F32)
    rest = x - first
    second = rest.astype(BF16).astype(F32)
    return first, second, rest - second


def by_lane(x, count):
    lane = lax.broadcasted_iota(jnp.int32, x.shape, 1)
    first, second, third = split3(x)
    picked = jnp.where(lane < count, first, jnp.where(lane < 2 * count, second, third))
    return jnp.where(lane < 3 * count, picked, 0.0).astype(BF16)


def head_slot(shape, count):
    slot = lax.broadcasted_iota(jnp.int32, shape, 0)
    live = slot < 3 * count
    slot = slot - jnp.where(slot >= 2 * count, 2 * count, jnp.where(slot >= count, count, 0))
    return jnp.where(live, slot, -1)


def spread_matrix(first_head, width, count):
    shape = (LANES, width)
    head = first_head + lax.broadcasted_iota(jnp.int32, shape, 1) // P_SIZE
    return jnp.where(head_slot(shape, count) == head, 1.0, 0.0).astype(BF16)


def dot(a, b):
    return jnp.dot(a, b, preferred_element_type=F32)


def near_kernel(inner_w, state_w, near):
    near[...] = inner_w[0:RIM, 0:LANES] + state_w[0:RIM, 0:LANES]


def tail_kernel(below, above, own, near, tail):
    here = lax.axis_index("head")
    last = [x[x.shape[0] - RIM :, :] for x in (below, above, own)]
    tail[...] = jnp.where(here == 0, last[0], jnp.where(here == 2, last[1], last[2]))


def repeat_lanes(x):
    count = x.shape[1]
    lane = lax.broadcasted_iota(jnp.int32, (count, LANES), 1)
    slot = lax.broadcasted_iota(jnp.int32, (count, LANES), 0)
    hits = (lane == slot) | (lane == slot + count) | (lane == slot + 2 * count)
    copies = jnp.where(hits, 1.0, 0.0).astype(BF16)
    return sum(dot(part.astype(BF16), copies) for part in split3(x))


def block_kernel(
    lens_row,
    own,
    below,
    above,
    top,
    bottom,
    rim,
    rim_far,
    gain,
    step_w,
    step_bias,
    rate,
    taps_state,
    taps_inner,
    state_w,
    inner_w,
    normed_out,
    sent,
    conv_out,
    scaled_out,
    cum_out,
    cum_rows,
    scores_out,
    maps_out,
    head_decay_out,
    normed,
    local,
    *,
    heads_here,
):
    rows = own.shape[0]
    length = normed.shape[0] - RIM
    here = lax.axis_index("head")
    first = lax.axis_index("seq") * length

    def norm(x):
        x = x.astype(F32)
        mean = jnp.mean(x * x, axis=-1, keepdims=True)
        return (x * lax.rsqrt(mean + 1e-05) * gain[...]).astype(BF16)

    def put(owner, offset, x):
        start = pl.multiple_of(RIM + owner * rows + offset, RIM)
        normed[pl.ds(start, x.shape[0]), :] = norm(x)

    half = rows // 2
    put(here, 0, own[...])
    put((here + 3) % 4, 0, below[...])
    put((here + 1) % 4, 0, above[...])
    far = (here + 2) % 4
    put(far, 0, top[...])
    put(far, half, bottom[...])
    normed[0:RIM, :] = norm(rim[...] + rim_far[...])
    normed_out[...] = normed[RIM:, :]

    passages = lens_row.shape[1]
    up = lax.broadcasted_iota(jnp.int32, (passages, passages), 0)
    across = lax.broadcasted_iota(jnp.int32, (passages, passages), 1)
    lens = jnp.broadcast_to(lens_row[...].astype(F32), (8, passages))
    whole = jnp.floor(lens * (1.0 / 128.0))
    before = jnp.where(up < across, 1.0, 0.0).astype(BF16)
    starts_row = 128.0 * dot(whole.astype(BF16), before)
    starts_row = (starts_row + dot((lens - 128.0 * whole).astype(BF16), before))[0:1]
    starts_col = jnp.sum(
        jnp.where(across < up, lens_row[...].astype(F32), 0.0), axis=1, keepdims=True
    )
    base = first.astype(F32)
    pos = lax.broadcasted_iota(jnp.int32, (length + RIM, passages), 0).astype(F32)
    ids_pad = jnp.sum(
        jnp.where(pos + (base - RIM) >= starts_row, 1.0, 0.0), axis=1, keepdims=True
    )
    pos = lax.broadcasted_iota(jnp.int32, (passages, length), 1).astype(F32)
    ids_row = jnp.sum(jnp.where(pos + base >= starts_col, 1.0, 0.0), axis=0, keepdims=True)
    ids_wide = jnp.broadcast_to(ids_pad, (length + RIM, LANES))
    ids = ids_wide[RIM:]
    agree = [
        jnp.where(pltpu.roll(ids_wide, lag, 0)[RIM:] == ids, 1.0, 0.0) for lag in range(1, K)
    ]

    def conv(raw, taps):
        acc = taps[0:1] * raw[RIM:]
        for lag in range(1, K):
            moved = pltpu.roll(raw, lag, 0)[RIM:]
            same = jnp.concatenate([agree[lag - 1]] * (raw.shape[1] // LANES), axis=1)
            acc = acc + taps[lag : lag + 1] * moved * same
        return (acc * jax.nn.sigmoid(acc)).astype(BF16)

    x = lax.dot_general(
        normed[RIM:, :], step_w[...], (((1,), (1,)), ((), ())), preferred_element_type=F32
    )
    x = repeat_lanes(x + step_bias[...])
    rates = jnp.broadcast_to(rate[...].astype(F32) * 2.0 ** (-21), (8, rate.shape[1]))
    raw = dot(normed[...], state_w[...]).astype(BF16).astype(F32)
    maps = conv(raw, taps_state[...])
    maps_in = maps[:, :N]
    maps_out[...] = maps[:, N:]
    maps_in_t = maps_in.astype(F32).T.astype(BF16)
    t = lax.broadcasted_iota(jnp.int32, (length, length), 0)
    s = lax.broadcasted_iota(jnp.int32, (length, length), 1)
    ids_two = jnp.concatenate([ids] * (length // LANES), axis=1)
    mask = (ids_two == ids_row) & (t >= s)
    scores_out[...] = jnp.where(mask, dot(maps[:, N:], maps_in_t), 0.0)

    step = jnp.maximum(x, 0.0) + jnp.log1p(jnp.exp(-jnp.abs(x)))
    log_decay = -step * repeat_lanes(rates)[0:1]
    ones = jnp.where(t >= s, 1.0, 0.0).astype(BF16)
    cum = sum(dot(ones, part.astype(BF16)) for part in split3(log_decay))
    last = cum[length - 1 :, :]
    ids_last = ids[length - 1 :, :]
    prior = ids_wide[RIM - 1 : RIM, :]
    step3 = by_lane(step, heads_here)
    tail = jnp.exp(jnp.minimum(last - cum, 0.0)) * jnp.where(ids == ids_last, 1.0, 0.0)
    tail3 = by_lane(tail, heads_here)
    keep = jnp.exp(cum) * jnp.where(ids == prior, 1.0, 0.0)
    keep3 = by_lane(keep, heads_here)
    head_decay_out[...] = keep3
    cum_out[...] = by_lane(cum, heads_here)
    cum_rows[...] = cum.T

    raw = dot(normed[...], inner_w[...]).astype(BF16).astype(F32)
    mixed = conv(raw, taps_inner[...])
    conv_out[...] = mixed
    spread = spread_matrix(0, local.shape[1], heads_here)
    scaled = (mixed.astype(F32) * dot(step3, spread)).astype(BF16)
    scaled_out[...] = scaled
    tail_in = (dot(tail3, spread) * scaled.astype(F32)).astype(BF16)
    local[...] = dot(maps_in_t, tail_in)

    span = local.shape[1] // 2
    decay = jnp.broadcast_to(keep3[length - RIM :].astype(F32)[RIM - 1 :], (8, LANES))
    for piece in range(sent.shape[0]):
        group, side = piece // 2, piece % 2
        part = local[8 * group : 8 * group + 8, side * span : (side + 1) * span]
        sent[piece, :, 0:span] = part.astype(BF16)
        sent[piece, :, span:] = decay.astype(BF16)


def inside_kernel(
    normed,
    scaled,
    conv,
    cum,
    cum_rows,
    scores,
    skip,
    gate_w,
    inside,
    gate,
    *,
    heads_here,
):
    length = scaled.shape[0]
    half = length // 2
    per = CHUNK // P_SIZE
    lane = lax.broadcasted_iota(jnp.int32, (length, CHUNK), 1) // P_SIZE
    slots = head_slot((LANES, length), heads_here)
    skip3 = by_lane(repeat_lanes(jnp.broadcast_to(skip[...], (8, heads_here))), heads_here)
    for c in range(scaled.shape[1] // CHUNK):
        cols = slice(c * CHUNK, (c + 1) * CHUNK)
        x = scaled[:, cols]
        tops, bottoms, top_x, all_x = [], [], [], []
        for i in range(per):
            head = c * per + i
            pick = jnp.where(slots == head, 1.0, 0.0).astype(BF16)
            cum_t = dot(cum[...], pick)
            cum_s = cum_rows[head : head + 1, :]
            own = jnp.where(lane == i, x, jnp.zeros_like(x))
            upper = jnp.exp(jnp.minimum(cum_t[:half, :half] - cum_s[:, :half], 0.0))
            lower = jnp.exp(jnp.minimum(cum_t[half:] - cum_s, 0.0))
            tops.append((upper * scores[0:half, 0:half]).astype(BF16))
            bottoms.append((lower * scores[half:, :]).astype(BF16))
            top_x.append(own[:half])
            all_x.append(own)
        spread = spread_matrix(c * per, CHUNK, heads_here)
        skips = dot(skip3, spread)[0:1]
        upper = dot(jnp.concatenate(tops, axis=1), jnp.concatenate(top_x, axis=0))
        lower = dot(jnp.concatenate(bottoms, axis=1), jnp.concatenate(all_x, axis=0))
        inside[:, cols] = jnp.concatenate([upper, lower], axis=0) + (
            skips * conv[:, cols].astype(F32)
        )
        vals = dot(normed[...], gate_w[:, cols]).astype(BF16).astype(F32)
        gate[:, cols] = vals * jax.nn.sigmoid(vals)


def scan_kernel(got, back, *, heads_here):
    blocks, depth, width = got.shape
    span = width - LANES
    side = lax.axis_index("seq") % 2
    spread = spread_matrix(side * (span // P_SIZE), span, heads_here)
    parts = got[:, :, span:].astype(F32).reshape(blocks * depth, LANES).astype(BF16)
    decay = dot(parts, spread)
    state = jnp.zeros((depth, span), F32)
    for b in range(blocks):
        back[b] = state.astype(BF16)
        if b < blocks - 1:
            state = decay[b * depth : (b + 1) * depth] * state + got[b, :, 0:span].astype(F32)


def out_kernel(
    got,
    maps,
    head_decay,
    inside,
    gate,
    norm_gain,
    out_w,
    out0,
    out1,
    out2,
    out2b,
    out3,
    states,
    x,
    sums,
    *,
    heads_here,
):
    length = inside.shape[0]
    rows = length // 4
    half = rows // 2
    here = lax.axis_index("head")
    span = got.shape[2]
    for piece in range(got.shape[0]):
        group, side = piece // 2, piece % 2
        states[8 * group : 8 * group + 8, side * span : (side + 1) * span] = got[piece].astype(
            F32
        )
    total = jnp.zeros((length, 1), F32)
    for c in range(inside.shape[1] // CHUNK):
        cols = slice(c * CHUNK, (c + 1) * CHUNK)
        spread = spread_matrix(c * (CHUNK // P_SIZE), CHUNK, heads_here)
        carried = dot(maps[...], states[:, cols].astype(BF16)) * dot(head_decay[...], spread)
        gated = (inside[:, cols] + carried) * gate[:, cols]
        total = total + jnp.sum(gated * gated, axis=1, keepdims=True)
        ready = (gated * norm_gain[:, cols]).astype(BF16)
        for b in range(4):
            start = pl.multiple_of(((b + 4 - here) % 4) * rows, rows)
            x[pl.ds(start, rows), cols] = ready[b * rows : (b + 1) * rows]
    packed = by_lane(jnp.broadcast_to(total, (length, LANES)), 1)
    for b in range(4):
        start = pl.multiple_of(((b + 4 - here) % 4) * rows, rows)
        sums[pl.ds(start, rows), :] = packed[b * rows : (b + 1) * rows]

    def put(cols, part):
        out0[:, cols] = part[0:rows]
        out1[:, cols] = part[rows : 2 * rows]
        out2[:, cols] = part[2 * rows : 2 * rows + half]
        out2b[:, cols] = part[2 * rows + half : 3 * rows]
        out3[:, cols] = part[3 * rows :]

    width = out_w.shape[1]
    for c in range(width // WIDE):
        cols = slice(c * WIDE, (c + 1) * WIDE)
        put(cols, dot(x[...], out_w[:, cols]).astype(BF16))
    put(slice(width, width + LANES), sums[...])


def close_kernel(own, one, two, two_b, three, mixed):
    width = mixed.shape[1]
    half = two.shape[0]
    for i, far in enumerate((two, two_b)):
        rows = slice(i * half, (i + 1) * half)
        total = own[rows, :].astype(F32) + one[rows, :].astype(F32)
        total = total + far[...].astype(F32) + three[rows, :].astype(F32)
        mean = jnp.sum(total[:, width:], axis=1, keepdims=True) / (H * P_SIZE)
        mixed[rows, :] = (total[:, :width] * lax.rsqrt(mean + 1e-05)).astype(BF16)


def vmem():
    return pl.BlockSpec(memory_space=pltpu.VMEM)


def call(kernel, name, in_specs, out_shape, scratch_shapes, limit):
    return pl.pallas_call(
        kernel,
        in_specs=in_specs,
        out_specs=[vmem()] * len(out_shape),
        out_shape=out_shape,
        scratch_shapes=scratch_shapes,
        compiler_params=pltpu.CompilerParams(vmem_limit_bytes=limit << 20),
        name=name,
    )


def on_device(
    tokens,
    input_gain,
    gate_weight,
    inner_weight,
    state_weight,
    step_weight,
    step_bias,
    decay_exponent,
    conv_inner,
    conv_state,
    skip_gain,
    norm_gain,
    out_weight,
    passage_lengths,
):
    rows, width = tokens.shape
    heads = lax.axis_size("head")
    blocks = lax.axis_size("seq")
    heads_here = step_weight.shape[1]
    channels = heads_here * P_SIZE
    length = heads * rows
    passages = passage_lengths.shape[0]
    span = channels // 2
    below, above, top, bottom, rim, rim_far = gather_tokens(tokens, inner_weight, state_weight)

    def shape(dims, kind):
        return jax.ShapeDtypeStruct(dims, kind)

    normed, sent, conv, scaled, cum, cum_rows, scores, maps, head_decay = call(
        lambda *refs: block_kernel(*refs, heads_here=heads_here),
        "block",
        [vmem()] * 16,
        [
            shape((length, width), BF16),
            shape((blocks, 8, span + LANES), BF16),
            shape((length, channels), BF16),
            shape((length, channels), BF16),
            shape((length, LANES), BF16),
            shape((LANES, length), F32),
            shape((length, length), F32),
            shape((length, N), BF16),
            shape((length, LANES), BF16),
        ],
        [
            pltpu.VMEM((length + RIM, width), BF16),
            pltpu.VMEM((N, channels), F32),
        ],
        BLOCK_LIMIT,
    )(
        passage_lengths[None],
        tokens,
        below,
        above,
        top,
        bottom,
        rim,
        rim_far,
        input_gain[None],
        step_weight.T,
        step_bias[None],
        decay_exponent[None],
        conv_state,
        conv_inner,
        state_weight,
        inner_weight,
    )

    inside, gate = call(
        lambda *refs: inside_kernel(*refs, heads_here=heads_here),
        "inside",
        [vmem()] * 8,
        [shape((length, channels), F32), shape((length, channels), F32)],
        [],
        INSIDE_LIMIT,
    )(normed, scaled, conv, cum, cum_rows, scores, skip_gain[None], gate_weight)
    sent, inside, gate, out_gain = lax.optimization_barrier(
        (sent, inside, gate, norm_gain[None])
    )
    got = lax.all_to_all(sent, "seq", 0, 0, tiled=True)

    (back,) = call(
        lambda *refs: scan_kernel(*refs, heads_here=heads_here),
        "scan",
        [vmem()],
        [shape((blocks, 8, span), BF16)],
        [],
        SMALL_LIMIT,
    )(got)
    states = lax.all_to_all(back, "seq", 0, 0, tiled=True)

    out_width = out_weight.shape[1]
    packed = out_width + LANES
    own, one, two, two_b, three = call(
        lambda *refs: out_kernel(*refs, heads_here=heads_here),
        "out",
        [vmem()] * 7,
        [shape((n, packed), BF16) for n in (rows, rows, rows // 2, rows // 2, rows)],
        [
            pltpu.VMEM((N, channels), F32),
            pltpu.VMEM((length, channels), BF16),
            pltpu.VMEM((length, LANES), BF16),
        ],
        OUT_LIMIT,
    )(states, maps, head_decay, inside, gate, out_gain, out_weight)
    (mixed,) = call(
        close_kernel,
        "close",
        [vmem()] * 5,
        [shape((rows, out_width), BF16)],
        [],
        SMALL_LIMIT,
    )(
        own,
        around(one, "head", 1),
        around(two, "head", 2),
        around(two_b, "head", 2),
        around(three, "head", 3),
    )
    return mixed


def solution(mesh):
    in_specs = (
        P(("seq", "head"), None),
        P(),
        P(None, "head"),
        P(None, "head"),
        P(),
        P(None, "head"),
        P("head"),
        P("head"),
        P(None, "head"),
        P(),
        P("head"),
        P("head"),
        P("head", None),
        P(),
    )
    out_specs = P(("seq", "head"), None)
    return jax.shard_map(
        on_device, mesh=mesh, in_specs=in_specs, out_specs=out_specs, check_vma=False
    )
```

```python
import jax
import jax.numpy as jnp
from jax import lax
from jax.experimental import pallas as pl
from jax.experimental.pallas import tpu as pltpu
from jax.sharding import PartitionSpec as P

H = 80
P_SIZE = 64
N = 128
K = 4
RIM = 16
LANES = 128
CHUNK = 256
WIDE = 512
BLOCK_LIMIT = 16
INSIDE_LIMIT = 16
OUT_LIMIT = 16
SMALL_LIMIT = 8
F32 = jnp.float32
BF16 = jnp.bfloat16


def around(block, axis, distance):
    size = lax.axis_size(axis)
    return lax.ppermute(block, axis, [(i, (i + distance) % size) for i in range(size)])


def gather_tokens(tokens, inner_weight, state_weight):
    heads = lax.axis_size("head")
    blocks = lax.axis_size("seq")
    rows, width = tokens.shape
    half = rows // 2
    first = tokens[:half]
    low = [around(first, "head", distance) for distance in (1, heads - 1, 2)]
    last = heads - 1
    route = [(s * heads + last, (s + 1) * heads) for s in range(blocks - 1)]
    rim = lax.ppermute(tokens[rows - RIM // 2 :], ("seq", "head"), route)
    (near,) = call(
        near_kernel,
        "near",
        [vmem()] * 2,
        [jax.ShapeDtypeStruct((RIM, LANES), tokens.dtype)],
        [],
        BLOCK_LIMIT,
    )(inner_weight, state_weight)
    (second,) = call(
        join_kernel,
        "join",
        [vmem()] * 2,
        [jax.ShapeDtypeStruct((half + RIM // 2, width), tokens.dtype)],
        [],
        SMALL_LIMIT,
    )(tokens, rim)
    high = [around(second, "head", distance) for distance in (1, heads - 1, 2)]
    return low, high, rim, near


def split3(x):
    first = x.astype(BF16).astype(F32)
    rest = x - first
    second = rest.astype(BF16).astype(F32)
    return first, second, rest - second


def by_lane(x, count):
    lane = lax.broadcasted_iota(jnp.int32, x.shape, 1)
    first, second, third = split3(x)
    picked = jnp.where(lane < count, first, jnp.where(lane < 2 * count, second, third))
    return jnp.where(lane < 3 * count, picked, 0.0).astype(BF16)


def head_slot(shape, count):
    slot = lax.broadcasted_iota(jnp.int32, shape, 0)
    live = slot < 3 * count
    slot = slot - jnp.where(slot >= 2 * count, 2 * count, jnp.where(slot >= count, count, 0))
    return jnp.where(live, slot, -1)


def spread_matrix(first_head, width, count):
    shape = (LANES, width)
    head = first_head + lax.broadcasted_iota(jnp.int32, shape, 1) // P_SIZE
    return jnp.where(head_slot(shape, count) == head, 1.0, 0.0).astype(BF16)


def dot(a, b):
    return jnp.dot(a, b, preferred_element_type=F32)


def near_kernel(inner_w, state_w, near):
    near[...] = inner_w[0:RIM, 0:LANES] + state_w[0:RIM, 0:LANES]


def join_kernel(own, rim, second):
    half = own.shape[0] // 2
    second[0:half, :] = own[half:, :]
    second[half:, :] = rim[...]


def repeat_lanes(x):
    count = x.shape[1]
    lane = lax.broadcasted_iota(jnp.int32, (count, LANES), 1)
    slot = lax.broadcasted_iota(jnp.int32, (count, LANES), 0)
    hits = (lane == slot) | (lane == slot + count) | (lane == slot + 2 * count)
    copies = jnp.where(hits, 1.0, 0.0).astype(BF16)
    return sum(dot(part.astype(BF16), copies) for part in split3(x))


def block_kernel(
    lens_row,
    own,
    below_low,
    above_low,
    far_low,
    below_high,
    above_high,
    far_high,
    rim,
    near,
    gain,
    step_w,
    step_bias,
    rate,
    taps_state,
    taps_inner,
    state_w,
    inner_w,
    normed_out,
    sent,
    conv_out,
    scaled_out,
    cum_out,
    cum_rows,
    scores_out,
    maps_out,
    head_decay_out,
    normed,
    local,
    *,
    heads_here,
):
    rows = own.shape[0]
    length = normed.shape[0] - RIM
    here = lax.axis_index("head")
    first = lax.axis_index("seq") * length

    def norm(x):
        x = x.astype(F32)
        mean = jnp.mean(x * x, axis=-1, keepdims=True)
        return (x * lax.rsqrt(mean + 1e-05) * gain[...]).astype(BF16)

    def put(owner, offset, x):
        start = pl.multiple_of(RIM + owner * rows + offset, RIM)
        normed[pl.ds(start, x.shape[0]), :] = norm(x)

    half = rows // 2
    put(here, 0, own[...])
    for step, low, high in (
        (3, below_low, below_high),
        (1, above_low, above_high),
        (2, far_low, far_high),
    ):
        owner = (here + step) % 4
        put(owner, 0, low[...])
        put(owner, half, high[0:half, :])
    tail = rim[...].astype(F32)
    for high in (below_high, above_high, far_high):
        tail = tail + high[half:, :].astype(F32)
    normed[0:RIM, :] = norm(jnp.concatenate([jnp.zeros_like(tail), tail], axis=0))
    normed_out[...] = normed[RIM:, :]

    passages = lens_row.shape[1]
    up = lax.broadcasted_iota(jnp.int32, (passages, passages), 0)
    across = lax.broadcasted_iota(jnp.int32, (passages, passages), 1)
    lens = jnp.broadcast_to(lens_row[...].astype(F32), (8, passages))
    whole = jnp.floor(lens * (1.0 / 128.0))
    before = jnp.where(up < across, 1.0, 0.0).astype(BF16)
    starts_row = 128.0 * dot(whole.astype(BF16), before)
    starts_row = (starts_row + dot((lens - 128.0 * whole).astype(BF16), before))[0:1]
    starts_col = jnp.sum(
        jnp.where(across < up, lens_row[...].astype(F32), 0.0), axis=1, keepdims=True
    )
    base = first.astype(F32)
    pos = lax.broadcasted_iota(jnp.int32, (length + RIM, passages), 0).astype(F32)
    ids_pad = jnp.sum(
        jnp.where(pos + (base - RIM) >= starts_row, 1.0, 0.0), axis=1, keepdims=True
    )
    pos = lax.broadcasted_iota(jnp.int32, (passages, length), 1).astype(F32)
    ids_row = jnp.sum(jnp.where(pos + base >= starts_col, 1.0, 0.0), axis=0, keepdims=True)
    ids_wide = jnp.broadcast_to(ids_pad, (length + RIM, LANES))
    ids = ids_wide[RIM:]
    agree = [
        jnp.where(pltpu.roll(ids_wide, lag, 0)[RIM:] == ids, 1.0, 0.0) for lag in range(1, K)
    ]

    def conv(raw, taps):
        acc = taps[0:1] * raw[RIM:]
        for lag in range(1, K):
            moved = pltpu.roll(raw, lag, 0)[RIM:]
            same = jnp.concatenate([agree[lag - 1]] * (raw.shape[1] // LANES), axis=1)
            acc = acc + taps[lag : lag + 1] * moved * same
        return (acc * jax.nn.sigmoid(acc)).astype(BF16)

    x = lax.dot_general(
        normed[RIM:, :], step_w[...], (((1,), (1,)), ((), ())), preferred_element_type=F32
    )
    x = repeat_lanes(x + step_bias[...])
    rates = jnp.broadcast_to(rate[...].astype(F32) * 2.0 ** (-21), (8, rate.shape[1]))
    raw = dot(normed[...], state_w[...]).astype(BF16).astype(F32)
    maps = conv(raw, taps_state[...])
    maps_in = maps[:, :N]
    maps_out[...] = maps[:, N:]
    maps_in_t = maps_in.astype(F32).T.astype(BF16)
    t = lax.broadcasted_iota(jnp.int32, (length, length), 0)
    s = lax.broadcasted_iota(jnp.int32, (length, length), 1)
    ids_two = jnp.concatenate([ids] * (length // LANES), axis=1)
    mask = (ids_two == ids_row) & (t >= s)
    scores_out[...] = jnp.where(mask, dot(maps[:, N:], maps_in_t), 0.0)

    step = jnp.maximum(x, 0.0) + jnp.log1p(jnp.exp(-jnp.abs(x)))
    log_decay = -step * repeat_lanes(rates)[0:1]
    ones = jnp.where(t >= s, 1.0, 0.0).astype(BF16)
    cum = sum(dot(ones, part.astype(BF16)) for part in split3(log_decay))
    last = cum[length - 1 :, :]
    ids_last = ids[length - 1 :, :]
    prior = ids_wide[RIM - 1 : RIM, :]
    step3 = by_lane(step, heads_here)
    tail = jnp.exp(jnp.minimum(last - cum, 0.0)) * jnp.where(ids == ids_last, 1.0, 0.0)
    tail3 = by_lane(tail, heads_here)
    keep = jnp.exp(cum) * jnp.where(ids == prior, 1.0, 0.0)
    keep3 = by_lane(keep, heads_here)
    head_decay_out[...] = keep3
    cum_out[...] = by_lane(cum, heads_here)
    cum_rows[...] = cum.T

    raw = dot(normed[...], inner_w[...]).astype(BF16).astype(F32)
    mixed = conv(raw, taps_inner[...])
    conv_out[...] = mixed
    spread = spread_matrix(0, local.shape[1], heads_here)
    scaled = (mixed.astype(F32) * dot(step3, spread)).astype(BF16)
    scaled_out[...] = scaled
    tail_in = (dot(tail3, spread) * scaled.astype(F32)).astype(BF16)
    local[...] = dot(maps_in_t, tail_in)

    span = local.shape[1] // 2
    decay = jnp.broadcast_to(keep3[length - RIM :].astype(F32)[RIM - 1 :], (8, LANES))
    for piece in range(sent.shape[0]):
        group, side = piece // 2, piece % 2
        part = local[8 * group : 8 * group + 8, side * span : (side + 1) * span]
        sent[piece, :, 0:span] = part.astype(BF16)
        sent[piece, :, span:] = decay.astype(BF16)


def inside_kernel(
    normed,
    scaled,
    conv,
    cum,
    cum_rows,
    scores,
    skip,
    gate_w,
    inside,
    gate,
    *,
    heads_here,
):
    length = scaled.shape[0]
    half = length // 2
    per = CHUNK // P_SIZE
    lane = lax.broadcasted_iota(jnp.int32, (length, CHUNK), 1) // P_SIZE
    slots = head_slot((LANES, length), heads_here)
    skip3 = by_lane(repeat_lanes(jnp.broadcast_to(skip[...], (8, heads_here))), heads_here)
    for c in range(scaled.shape[1] // CHUNK):
        cols = slice(c * CHUNK, (c + 1) * CHUNK)
        x = scaled[:, cols]
        tops, bottoms, top_x, all_x = [], [], [], []
        for i in range(per):
            head = c * per + i
            pick = jnp.where(slots == head, 1.0, 0.0).astype(BF16)
            cum_t = dot(cum[...], pick)
            cum_s = cum_rows[head : head + 1, :]
            own = jnp.where(lane == i, x, jnp.zeros_like(x))
            upper = jnp.exp(jnp.minimum(cum_t[:half, :half] - cum_s[:, :half], 0.0))
            lower = jnp.exp(jnp.minimum(cum_t[half:] - cum_s, 0.0))
            tops.append((upper * scores[0:half, 0:half]).astype(BF16))
            bottoms.append((lower * scores[half:, :]).astype(BF16))
            top_x.append(own[:half])
            all_x.append(own)
        spread = spread_matrix(c * per, CHUNK, heads_here)
        skips = dot(skip3, spread)[0:1]
        upper = dot(jnp.concatenate(tops, axis=1), jnp.concatenate(top_x, axis=0))
        lower = dot(jnp.concatenate(bottoms, axis=1), jnp.concatenate(all_x, axis=0))
        inside[:, cols] = jnp.concatenate([upper, lower], axis=0) + (
            skips * conv[:, cols].astype(F32)
        )
        vals = dot(normed[...], gate_w[:, cols]).astype(BF16).astype(F32)
        gate[:, cols] = vals * jax.nn.sigmoid(vals)


def scan_kernel(got, back, *, heads_here):
    blocks, depth, width = got.shape
    span = width - LANES
    side = lax.axis_index("seq") % 2
    spread = spread_matrix(side * (span // P_SIZE), span, heads_here)
    parts = got[:, :, span:].astype(F32).reshape(blocks * depth, LANES).astype(BF16)
    decay = dot(parts, spread)
    state = jnp.zeros((depth, span), F32)
    for b in range(blocks):
        back[b] = state.astype(BF16)
        if b < blocks - 1:
            state = decay[b * depth : (b + 1) * depth] * state + got[b, :, 0:span].astype(F32)


def out_kernel(
    got,
    maps,
    head_decay,
    inside,
    gate,
    norm_gain,
    out_w,
    out0,
    out1,
    out2,
    out2b,
    out3,
    states,
    x,
    sums,
    *,
    heads_here,
):
    length = inside.shape[0]
    rows = length // 4
    half = rows // 2
    here = lax.axis_index("head")
    span = got.shape[2]
    for piece in range(got.shape[0]):
        group, side = piece // 2, piece % 2
        states[8 * group : 8 * group + 8, side * span : (side + 1) * span] = got[piece].astype(
            F32
        )
    total = jnp.zeros((length, 1), F32)
    for c in range(inside.shape[1] // CHUNK):
        cols = slice(c * CHUNK, (c + 1) * CHUNK)
        spread = spread_matrix(c * (CHUNK // P_SIZE), CHUNK, heads_here)
        carried = dot(maps[...], states[:, cols].astype(BF16)) * dot(head_decay[...], spread)
        gated = (inside[:, cols] + carried) * gate[:, cols]
        total = total + jnp.sum(gated * gated, axis=1, keepdims=True)
        ready = (gated * norm_gain[:, cols]).astype(BF16)
        for b in range(4):
            start = pl.multiple_of(((b + 4 - here) % 4) * rows, rows)
            x[pl.ds(start, rows), cols] = ready[b * rows : (b + 1) * rows]
    packed = by_lane(jnp.broadcast_to(total, (length, LANES)), 1)
    for b in range(4):
        start = pl.multiple_of(((b + 4 - here) % 4) * rows, rows)
        sums[pl.ds(start, rows), :] = packed[b * rows : (b + 1) * rows]

    def put(cols, part):
        out0[:, cols] = part[0:rows]
        out1[:, cols] = part[rows : 2 * rows]
        out2[:, cols] = part[2 * rows : 2 * rows + half]
        out2b[:, cols] = part[2 * rows + half : 3 * rows]
        out3[:, cols] = part[3 * rows :]

    width = out_w.shape[1]
    for c in range(width // WIDE):
        cols = slice(c * WIDE, (c + 1) * WIDE)
        put(cols, dot(x[...], out_w[:, cols]).astype(BF16))
    put(slice(width, width + LANES), sums[...])


def close_kernel(own, one, two, two_b, three, mixed):
    width = mixed.shape[1]
    half = two.shape[0]
    for i, far in enumerate((two, two_b)):
        rows = slice(i * half, (i + 1) * half)
        total = own[rows, :].astype(F32) + one[rows, :].astype(F32)
        total = total + far[...].astype(F32) + three[rows, :].astype(F32)
        mean = jnp.sum(total[:, width:], axis=1, keepdims=True) / (H * P_SIZE)
        mixed[rows, :] = (total[:, :width] * lax.rsqrt(mean + 1e-05)).astype(BF16)


def vmem():
    return pl.BlockSpec(memory_space=pltpu.VMEM)


def call(kernel, name, in_specs, out_shape, scratch_shapes, limit):
    return pl.pallas_call(
        kernel,
        in_specs=in_specs,
        out_specs=[vmem()] * len(out_shape),
        out_shape=out_shape,
        scratch_shapes=scratch_shapes,
        compiler_params=pltpu.CompilerParams(vmem_limit_bytes=limit << 20),
        name=name,
    )


def on_device(
    tokens,
    input_gain,
    gate_weight,
    inner_weight,
    state_weight,
    step_weight,
    step_bias,
    decay_exponent,
    conv_inner,
    conv_state,
    skip_gain,
    norm_gain,
    out_weight,
    passage_lengths,
):
    rows, width = tokens.shape
    heads = lax.axis_size("head")
    blocks = lax.axis_size("seq")
    heads_here = step_weight.shape[1]
    channels = heads_here * P_SIZE
    length = heads * rows
    passages = passage_lengths.shape[0]
    span = channels // 2
    low, high, rim, near = gather_tokens(tokens, inner_weight, state_weight)

    def shape(dims, kind):
        return jax.ShapeDtypeStruct(dims, kind)

    normed, sent, conv, scaled, cum, cum_rows, scores, maps, head_decay = call(
        lambda *refs: block_kernel(*refs, heads_here=heads_here),
        "block",
        [vmem()] * 18,
        [
            shape((length, width), BF16),
            shape((blocks, 8, span + LANES), BF16),
            shape((length, channels), BF16),
            shape((length, channels), BF16),
            shape((length, LANES), BF16),
            shape((LANES, length), F32),
            shape((length, length), F32),
            shape((length, N), BF16),
            shape((length, LANES), BF16),
        ],
        [
            pltpu.VMEM((length + RIM, width), BF16),
            pltpu.VMEM((N, channels), F32),
        ],
        BLOCK_LIMIT,
    )(
        passage_lengths[None],
        tokens,
        *low,
        *high,
        rim,
        near,
        input_gain[None],
        step_weight.T,
        step_bias[None],
        decay_exponent[None],
        conv_state,
        conv_inner,
        state_weight,
        inner_weight,
    )

    inside, gate = call(
        lambda *refs: inside_kernel(*refs, heads_here=heads_here),
        "inside",
        [vmem()] * 8,
        [shape((length, channels), F32), shape((length, channels), F32)],
        [],
        INSIDE_LIMIT,
    )(normed, scaled, conv, cum, cum_rows, scores, skip_gain[None], gate_weight)
    sent, inside, gate, out_gain = lax.optimization_barrier(
        (sent, inside, gate, norm_gain[None])
    )
    got = lax.all_to_all(sent, "seq", 0, 0, tiled=True)

    (back,) = call(
        lambda *refs: scan_kernel(*refs, heads_here=heads_here),
        "scan",
        [vmem()],
        [shape((blocks, 8, span), BF16)],
        [],
        SMALL_LIMIT,
    )(got)
    states = lax.all_to_all(back, "seq", 0, 0, tiled=True)

    out_width = out_weight.shape[1]
    packed = out_width + LANES
    own, one, two, two_b, three = call(
        lambda *refs: out_kernel(*refs, heads_here=heads_here),
        "out",
        [vmem()] * 7,
        [shape((n, packed), BF16) for n in (rows, rows, rows // 2, rows // 2, rows)],
        [
            pltpu.VMEM((N, channels), F32),
            pltpu.VMEM((length, channels), BF16),
            pltpu.VMEM((length, LANES), BF16),
        ],
        OUT_LIMIT,
    )(states, maps, head_decay, inside, gate, out_gain, out_weight)
    (mixed,) = call(
        close_kernel,
        "close",
        [vmem()] * 5,
        [shape((rows, out_width), BF16)],
        [],
        SMALL_LIMIT,
    )(
        own,
        around(one, "head", 1),
        around(two, "head", 2),
        around(two_b, "head", 2),
        around(three, "head", 3),
    )
    return mixed


def solution(mesh):
    in_specs = (
        P(("seq", "head"), None),
        P(),
        P(None, "head"),
        P(None, "head"),
        P(),
        P(None, "head"),
        P("head"),
        P("head"),
        P(None, "head"),
        P(),
        P("head"),
        P("head"),
        P("head", None),
        P(),
    )
    out_specs = P(("seq", "head"), None)
    return jax.shard_map(
        on_device, mesh=mesh, in_specs=in_specs, out_specs=out_specs, check_vma=False
    )
```

```python
import jax
import jax.numpy as jnp
from jax import lax
from jax.experimental import pallas as pl
from jax.experimental.pallas import tpu as pltpu
from jax.sharding import PartitionSpec as P

H = 80
P_SIZE = 64
N = 128
K = 4
RIM = 16
LANES = 128
CHUNK = 256
WIDE = 512
BLOCK_LIMIT = 16
INSIDE_LIMIT = 16
OUT_LIMIT = 16
SMALL_LIMIT = 8
F32 = jnp.float32
BF16 = jnp.bfloat16


def around(block, axis, distance):
    size = lax.axis_size(axis)
    return lax.ppermute(block, axis, [(i, (i + distance) % size) for i in range(size)])


def gather_tokens(tokens, inner_weight, state_weight, gate_weight):
    heads = lax.axis_size("head")
    blocks = lax.axis_size("seq")
    rows, width = tokens.shape
    half = rows // 2
    below = around(tokens, "head", 1)
    above = around(tokens, "head", heads - 1)
    bottom = around(tokens[half:], "head", 2)
    top = around(tokens[:half], "head", 2)
    last = heads - 1
    far = [(s * heads + last, (s + 1) * heads + 1) for s in range(blocks - 1)]
    rim_far = lax.ppermute(tokens[rows - RIM :], ("seq", "head"), far)
    (near,) = call(
        near_kernel,
        "near",
        [vmem()] * 3,
        [jax.ShapeDtypeStruct((RIM, LANES), tokens.dtype)],
        [],
        BLOCK_LIMIT,
    )(inner_weight, state_weight, gate_weight)
    (tail,) = call(
        tail_kernel,
        "tail",
        [vmem()] * 4,
        [jax.ShapeDtypeStruct((RIM, width), tokens.dtype)],
        [],
        SMALL_LIMIT,
    )(below, above, tokens, near)
    route = [
        (s * heads + h, (s + 1) * heads + h)
        for s in range(blocks - 1)
        for h in range(heads)
        if h != 1
    ]
    return below, above, top, bottom, lax.ppermute(tail, ("seq", "head"), route), rim_far


def split3(x):
    first = x.astype(BF16).astype(F32)
    rest = x - first
    second = rest.astype(BF16).astype(F32)
    return first, second, rest - second


def by_lane(x, count):
    lane = lax.broadcasted_iota(jnp.int32, x.shape, 1)
    first, second, third = split3(x)
    picked = jnp.where(lane < count, first, jnp.where(lane < 2 * count, second, third))
    return jnp.where(lane < 3 * count, picked, 0.0).astype(BF16)


def head_slot(shape, count):
    slot = lax.broadcasted_iota(jnp.int32, shape, 0)
    live = slot < 3 * count
    slot = slot - jnp.where(slot >= 2 * count, 2 * count, jnp.where(slot >= count, count, 0))
    return jnp.where(live, slot, -1)


def spread_matrix(first_head, width, count):
    shape = (LANES, width)
    head = first_head + lax.broadcasted_iota(jnp.int32, shape, 1) // P_SIZE
    return jnp.where(head_slot(shape, count) == head, 1.0, 0.0).astype(BF16)


def dot(a, b):
    return jnp.dot(a, b, preferred_element_type=F32)


def near_kernel(inner_w, state_w, gate_w, near):
    near[...] = (
        inner_w[0:RIM, 0:LANES] + state_w[0:RIM, 0:LANES] + gate_w[0:RIM, 0:LANES]
    )


def tail_kernel(below, above, own, near, tail):
    here = lax.axis_index("head")
    last = [x[x.shape[0] - RIM :, :] for x in (below, above, own)]
    tail[...] = jnp.where(here == 0, last[0], jnp.where(here == 2, last[1], last[2]))


def repeat_lanes(x):
    count = x.shape[1]
    lane = lax.broadcasted_iota(jnp.int32, (count, LANES), 1)
    slot = lax.broadcasted_iota(jnp.int32, (count, LANES), 0)
    hits = (lane == slot) | (lane == slot + count) | (lane == slot + 2 * count)
    copies = jnp.where(hits, 1.0, 0.0).astype(BF16)
    return sum(dot(part.astype(BF16), copies) for part in split3(x))


def norm_rows(x, gain):
    x = x.astype(F32)
    mean = jnp.mean(x * x, axis=-1, keepdims=True)
    return (x * lax.rsqrt(mean + 1e-05) * gain).astype(BF16)


def project_kernel(
    own,
    below,
    above,
    top,
    bottom,
    gain,
    step_w,
    state_w,
    inner_w,
    gate_w,
    step_raw,
    state_raw,
    inner_raw,
    gate,
    normed,
):
    rows = own.shape[0]
    half = rows // 2
    here = lax.axis_index("head")

    def put(owner, offset, x):
        start = pl.multiple_of(owner * rows + offset, half)
        normed[pl.ds(start, x.shape[0]), :] = norm_rows(x[...], gain[...])

    far = (here + 2) % 4
    put(here, 0, own)
    put((here + 3) % 4, 0, below)
    put((here + 1) % 4, 0, above)
    put(far, 0, top)
    put(far, half, bottom)
    step_raw[...] = lax.dot_general(
        normed[...], step_w[...], (((1,), (1,)), ((), ())), preferred_element_type=F32
    )
    state_raw[...] = dot(normed[...], state_w[...]).astype(BF16)
    inner_raw[...] = dot(normed[...], inner_w[...]).astype(BF16)
    for c in range(gate.shape[1] // CHUNK):
        cols = slice(c * CHUNK, (c + 1) * CHUNK)
        vals = dot(normed[...], gate_w[:, cols]).astype(BF16).astype(F32)
        gate[:, cols] = vals * jax.nn.sigmoid(vals)


def block_kernel(
    lens_row,
    rim,
    rim_far,
    gain,
    step_raw,
    state_raw,
    inner_raw,
    step_bias,
    rate,
    taps_state,
    taps_inner,
    state_w,
    inner_w,
    sent,
    conv_out,
    scaled_out,
    cum_out,
    cum_rows,
    scores_out,
    maps_out,
    head_decay_out,
    local,
    *,
    heads_here,
):
    length = inner_raw.shape[0]
    first = lax.axis_index("seq") * length
    rim_rows = norm_rows(rim[...] + rim_far[...], gain[...])

    def behind(weight, raw):
        before = dot(rim_rows, weight[...]).astype(BF16).astype(F32)
        return jnp.concatenate([before, raw[...].astype(F32)], axis=0)

    passages = lens_row.shape[1]
    up = lax.broadcasted_iota(jnp.int32, (passages, passages), 0)
    across = lax.broadcasted_iota(jnp.int32, (passages, passages), 1)
    lens = jnp.broadcast_to(lens_row[...].astype(F32), (8, passages))
    whole = jnp.floor(lens * (1.0 / 128.0))
    before = jnp.where(up < across, 1.0, 0.0).astype(BF16)
    starts_row = 128.0 * dot(whole.astype(BF16), before)
    starts_row = (starts_row + dot((lens - 128.0 * whole).astype(BF16), before))[0:1]
    starts_col = jnp.sum(
        jnp.where(across < up, lens_row[...].astype(F32), 0.0), axis=1, keepdims=True
    )
    base = first.astype(F32)
    pos = lax.broadcasted_iota(jnp.int32, (length + RIM, passages), 0).astype(F32)
    ids_pad = jnp.sum(
        jnp.where(pos + (base - RIM) >= starts_row, 1.0, 0.0), axis=1, keepdims=True
    )
    pos = lax.broadcasted_iota(jnp.int32, (passages, length), 1).astype(F32)
    ids_row = jnp.sum(jnp.where(pos + base >= starts_col, 1.0, 0.0), axis=0, keepdims=True)
    ids_wide = jnp.broadcast_to(ids_pad, (length + RIM, LANES))
    ids = ids_wide[RIM:]
    agree = [
        jnp.where(pltpu.roll(ids_wide, lag, 0)[RIM:] == ids, 1.0, 0.0) for lag in range(1, K)
    ]

    def conv(raw, taps):
        acc = taps[0:1] * raw[RIM:]
        for lag in range(1, K):
            moved = pltpu.roll(raw, lag, 0)[RIM:]
            same = jnp.concatenate([agree[lag - 1]] * (raw.shape[1] // LANES), axis=1)
            acc = acc + taps[lag : lag + 1] * moved * same
        return (acc * jax.nn.sigmoid(acc)).astype(BF16)

    x = repeat_lanes(step_raw[...] + step_bias[...])
    rates = jnp.broadcast_to(rate[...].astype(F32) * 2.0 ** (-21), (8, rate.shape[1]))
    raw = behind(state_w, state_raw)
    maps = conv(raw, taps_state[...])
    maps_in = maps[:, :N]
    maps_out[...] = maps[:, N:]
    maps_in_t = maps_in.astype(F32).T.astype(BF16)
    t = lax.broadcasted_iota(jnp.int32, (length, length), 0)
    s = lax.broadcasted_iota(jnp.int32, (length, length), 1)
    ids_two = jnp.concatenate([ids] * (length // LANES), axis=1)
    mask = (ids_two == ids_row) & (t >= s)
    scores_out[...] = jnp.where(mask, dot(maps[:, N:], maps_in_t), 0.0)

    step = jnp.maximum(x, 0.0) + jnp.log1p(jnp.exp(-jnp.abs(x)))
    log_decay = -step * repeat_lanes(rates)[0:1]
    ones = jnp.where(t >= s, 1.0, 0.0).astype(BF16)
    cum = sum(dot(ones, part.astype(BF16)) for part in split3(log_decay))
    last = cum[length - 1 :, :]
    ids_last = ids[length - 1 :, :]
    prior = ids_wide[RIM - 1 : RIM, :]
    step3 = by_lane(step, heads_here)
    tail = jnp.exp(jnp.minimum(last - cum, 0.0)) * jnp.where(ids == ids_last, 1.0, 0.0)
    tail3 = by_lane(tail, heads_here)
    keep = jnp.exp(cum) * jnp.where(ids == prior, 1.0, 0.0)
    keep3 = by_lane(keep, heads_here)
    head_decay_out[...] = keep3
    cum_out[...] = by_lane(cum, heads_here)
    cum_rows[...] = cum.T

    raw = behind(inner_w, inner_raw)
    mixed = conv(raw, taps_inner[...])
    conv_out[...] = mixed
    spread = spread_matrix(0, local.shape[1], heads_here)
    scaled = (mixed.astype(F32) * dot(step3, spread)).astype(BF16)
    scaled_out[...] = scaled
    tail_in = (dot(tail3, spread) * scaled.astype(F32)).astype(BF16)
    local[...] = dot(maps_in_t, tail_in)

    span = local.shape[1] // 2
    decay = jnp.broadcast_to(keep3[length - RIM :].astype(F32)[RIM - 1 :], (8, LANES))
    for piece in range(sent.shape[0]):
        group, side = piece // 2, piece % 2
        part = local[8 * group : 8 * group + 8, side * span : (side + 1) * span]
        sent[piece, :, 0:span] = part.astype(BF16)
        sent[piece, :, span:] = decay.astype(BF16)


def inside_kernel(
    scaled,
    conv,
    cum,
    cum_rows,
    scores,
    skip,
    inside,
    *,
    heads_here,
):
    length = scaled.shape[0]
    half = length // 2
    per = CHUNK // P_SIZE
    lane = lax.broadcasted_iota(jnp.int32, (length, CHUNK), 1) // P_SIZE
    slots = head_slot((LANES, length), heads_here)
    skip3 = by_lane(repeat_lanes(jnp.broadcast_to(skip[...], (8, heads_here))), heads_here)
    for c in range(scaled.shape[1] // CHUNK):
        cols = slice(c * CHUNK, (c + 1) * CHUNK)
        x = scaled[:, cols]
        tops, bottoms, top_x, all_x = [], [], [], []
        for i in range(per):
            head = c * per + i
            pick = jnp.where(slots == head, 1.0, 0.0).astype(BF16)
            cum_t = dot(cum[...], pick)
            cum_s = cum_rows[head : head + 1, :]
            own = jnp.where(lane == i, x, jnp.zeros_like(x))
            upper = jnp.exp(jnp.minimum(cum_t[:half, :half] - cum_s[:, :half], 0.0))
            lower = jnp.exp(jnp.minimum(cum_t[half:] - cum_s, 0.0))
            tops.append((upper * scores[0:half, 0:half]).astype(BF16))
            bottoms.append((lower * scores[half:, :]).astype(BF16))
            top_x.append(own[:half])
            all_x.append(own)
        spread = spread_matrix(c * per, CHUNK, heads_here)
        skips = dot(skip3, spread)[0:1]
        upper = dot(jnp.concatenate(tops, axis=1), jnp.concatenate(top_x, axis=0))
        lower = dot(jnp.concatenate(bottoms, axis=1), jnp.concatenate(all_x, axis=0))
        inside[:, cols] = jnp.concatenate([upper, lower], axis=0) + (
            skips * conv[:, cols].astype(F32)
        )


def scan_kernel(got, back, *, heads_here):
    blocks, depth, width = got.shape
    span = width - LANES
    side = lax.axis_index("seq") % 2
    spread = spread_matrix(side * (span // P_SIZE), span, heads_here)
    parts = got[:, :, span:].astype(F32).reshape(blocks * depth, LANES).astype(BF16)
    decay = dot(parts, spread)
    state = jnp.zeros((depth, span), F32)
    for b in range(blocks):
        back[b] = state.astype(BF16)
        if b < blocks - 1:
            state = decay[b * depth : (b + 1) * depth] * state + got[b, :, 0:span].astype(F32)


def out_kernel(
    got,
    maps,
    head_decay,
    inside,
    gate,
    norm_gain,
    out_w,
    out0,
    out1,
    out2,
    out2b,
    out3,
    states,
    x,
    sums,
    *,
    heads_here,
):
    length = inside.shape[0]
    rows = length // 4
    half = rows // 2
    here = lax.axis_index("head")
    span = got.shape[2]
    for piece in range(got.shape[0]):
        group, side = piece // 2, piece % 2
        states[8 * group : 8 * group + 8, side * span : (side + 1) * span] = got[piece].astype(
            F32
        )
    total = jnp.zeros((length, 1), F32)
    for c in range(inside.shape[1] // CHUNK):
        cols = slice(c * CHUNK, (c + 1) * CHUNK)
        spread = spread_matrix(c * (CHUNK // P_SIZE), CHUNK, heads_here)
        carried = dot(maps[...], states[:, cols].astype(BF16)) * dot(head_decay[...], spread)
        gated = (inside[:, cols] + carried) * gate[:, cols]
        total = total + jnp.sum(gated * gated, axis=1, keepdims=True)
        ready = (gated * norm_gain[:, cols]).astype(BF16)
        for b in range(4):
            start = pl.multiple_of(((b + 4 - here) % 4) * rows, rows)
            x[pl.ds(start, rows), cols] = ready[b * rows : (b + 1) * rows]
    packed = by_lane(jnp.broadcast_to(total, (length, LANES)), 1)
    for b in range(4):
        start = pl.multiple_of(((b + 4 - here) % 4) * rows, rows)
        sums[pl.ds(start, rows), :] = packed[b * rows : (b + 1) * rows]

    def put(cols, part):
        out0[:, cols] = part[0:rows]
        out1[:, cols] = part[rows : 2 * rows]
        out2[:, cols] = part[2 * rows : 2 * rows + half]
        out2b[:, cols] = part[2 * rows + half : 3 * rows]
        out3[:, cols] = part[3 * rows :]

    width = out_w.shape[1]
    for c in range(width // WIDE):
        cols = slice(c * WIDE, (c + 1) * WIDE)
        put(cols, dot(x[...], out_w[:, cols]).astype(BF16))
    put(slice(width, width + LANES), sums[...])


def close_kernel(own, one, two, two_b, three, mixed):
    width = mixed.shape[1]
    half = two.shape[0]
    for i, far in enumerate((two, two_b)):
        rows = slice(i * half, (i + 1) * half)
        total = own[rows, :].astype(F32) + one[rows, :].astype(F32)
        total = total + far[...].astype(F32) + three[rows, :].astype(F32)
        mean = jnp.sum(total[:, width:], axis=1, keepdims=True) / (H * P_SIZE)
        mixed[rows, :] = (total[:, :width] * lax.rsqrt(mean + 1e-05)).astype(BF16)


def vmem():
    return pl.BlockSpec(memory_space=pltpu.VMEM)


def call(kernel, name, in_specs, out_shape, scratch_shapes, limit):
    return pl.pallas_call(
        kernel,
        in_specs=in_specs,
        out_specs=[vmem()] * len(out_shape),
        out_shape=out_shape,
        scratch_shapes=scratch_shapes,
        compiler_params=pltpu.CompilerParams(vmem_limit_bytes=limit << 20),
        name=name,
    )


def on_device(
    tokens,
    input_gain,
    gate_weight,
    inner_weight,
    state_weight,
    step_weight,
    step_bias,
    decay_exponent,
    conv_inner,
    conv_state,
    skip_gain,
    norm_gain,
    out_weight,
    passage_lengths,
):
    rows, width = tokens.shape
    heads = lax.axis_size("head")
    blocks = lax.axis_size("seq")
    heads_here = step_weight.shape[1]
    channels = heads_here * P_SIZE
    length = heads * rows
    passages = passage_lengths.shape[0]
    span = channels // 2
    below, above, top, bottom, rim, rim_far = gather_tokens(
        tokens, inner_weight, state_weight, gate_weight
    )

    def shape(dims, kind):
        return jax.ShapeDtypeStruct(dims, kind)

    gain = input_gain[None]
    step_raw, state_raw, inner_raw, gate = call(
        project_kernel,
        "project",
        [vmem()] * 10,
        [
            shape((length, heads_here), F32),
            shape((length, 2 * N), BF16),
            shape((length, channels), BF16),
            shape((length, channels), F32),
        ],
        [pltpu.VMEM((length, width), BF16)],
        BLOCK_LIMIT,
    )(
        tokens,
        below,
        above,
        top,
        bottom,
        gain,
        step_weight.T,
        state_weight,
        inner_weight,
        gate_weight,
    )
    sent, conv, scaled, cum, cum_rows, scores, maps, head_decay = call(
        lambda *refs: block_kernel(*refs, heads_here=heads_here),
        "block",
        [vmem()] * 13,
        [
            shape((blocks, 8, span + LANES), BF16),
            shape((length, channels), BF16),
            shape((length, channels), BF16),
            shape((length, LANES), BF16),
            shape((LANES, length), F32),
            shape((length, length), F32),
            shape((length, N), BF16),
            shape((length, LANES), BF16),
        ],
        [pltpu.VMEM((N, channels), F32)],
        BLOCK_LIMIT,
    )(
        passage_lengths[None],
        rim,
        rim_far,
        gain,
        step_raw,
        state_raw,
        inner_raw,
        step_bias[None],
        decay_exponent[None],
        conv_state,
        conv_inner,
        state_weight,
        inner_weight,
    )

    (inside,) = call(
        lambda *refs: inside_kernel(*refs, heads_here=heads_here),
        "inside",
        [vmem()] * 6,
        [shape((length, channels), F32)],
        [],
        INSIDE_LIMIT,
    )(scaled, conv, cum, cum_rows, scores, skip_gain[None])
    sent, inside, gate, out_gain = lax.optimization_barrier(
        (sent, inside, gate, norm_gain[None])
    )
    got = lax.all_to_all(sent, "seq", 0, 0, tiled=True)

    (back,) = call(
        lambda *refs: scan_kernel(*refs, heads_here=heads_here),
        "scan",
        [vmem()],
        [shape((blocks, 8, span), BF16)],
        [],
        SMALL_LIMIT,
    )(got)
    states = lax.all_to_all(back, "seq", 0, 0, tiled=True)

    out_width = out_weight.shape[1]
    packed = out_width + LANES
    own, one, two, two_b, three = call(
        lambda *refs: out_kernel(*refs, heads_here=heads_here),
        "out",
        [vmem()] * 7,
        [shape((n, packed), BF16) for n in (rows, rows, rows // 2, rows // 2, rows)],
        [
            pltpu.VMEM((N, channels), F32),
            pltpu.VMEM((length, channels), BF16),
            pltpu.VMEM((length, LANES), BF16),
        ],
        OUT_LIMIT,
    )(states, maps, head_decay, inside, gate, out_gain, out_weight)
    (mixed,) = call(
        close_kernel,
        "close",
        [vmem()] * 5,
        [shape((rows, out_width), BF16)],
        [],
        SMALL_LIMIT,
    )(
        own,
        around(one, "head", 1),
        around(two, "head", 2),
        around(two_b, "head", 2),
        around(three, "head", 3),
    )
    return mixed


def solution(mesh):
    in_specs = (
        P(("seq", "head"), None),
        P(),
        P(None, "head"),
        P(None, "head"),
        P(),
        P(None, "head"),
        P("head"),
        P("head"),
        P(None, "head"),
        P(),
        P("head"),
        P("head"),
        P("head", None),
        P(),
    )
    out_specs = P(("seq", "head"), None)
    return jax.shard_map(
        on_device, mesh=mesh, in_specs=in_specs, out_specs=out_specs, check_vma=False
    )
```

```python
import jax
import jax.numpy as jnp
from jax import lax
from jax.experimental import pallas as pl
from jax.experimental.pallas import tpu as pltpu
from jax.sharding import PartitionSpec as P

H = 80
P_SIZE = 64
N = 128
K = 4
RIM = 16
LANES = 128
CHUNK = 256
WIDE = 512
BLOCK_LIMIT = 16
INSIDE_LIMIT = 16
OUT_LIMIT = 16
SMALL_LIMIT = 8
F32 = jnp.float32
BF16 = jnp.bfloat16


def around(block, axis, distance):
    size = lax.axis_size(axis)
    return lax.ppermute(block, axis, [(i, (i + distance) % size) for i in range(size)])


def gather_tokens(tokens, inner_weight, state_weight, gate_weight):
    heads = lax.axis_size("head")
    blocks = lax.axis_size("seq")
    rows, width = tokens.shape
    half = rows // 2
    below = around(tokens, "head", 1)
    above = around(tokens, "head", heads - 1)
    bottom = around(tokens[half:], "head", 2)
    top = around(tokens[:half], "head", 2)
    last = heads - 1
    far = [(s * heads + last, (s + 1) * heads + 1) for s in range(blocks - 1)]
    rim_far = lax.ppermute(tokens[rows - RIM :], ("seq", "head"), far)
    (near,) = call(
        near_kernel,
        "near",
        [vmem()] * 3,
        [jax.ShapeDtypeStruct((RIM, LANES), tokens.dtype)],
        [],
        BLOCK_LIMIT,
    )(inner_weight, state_weight, gate_weight)
    (tail,) = call(
        tail_kernel,
        "tail",
        [vmem()] * 4,
        [jax.ShapeDtypeStruct((RIM, width), tokens.dtype)],
        [],
        SMALL_LIMIT,
    )(below, above, tokens, near)
    route = [
        (s * heads + h, (s + 1) * heads + h)
        for s in range(blocks - 1)
        for h in range(heads)
        if h != 1
    ]
    return below, above, top, bottom, lax.ppermute(tail, ("seq", "head"), route), rim_far


def split3(x):
    first = x.astype(BF16).astype(F32)
    rest = x - first
    second = rest.astype(BF16).astype(F32)
    return first, second, rest - second


def by_lane(x, count):
    lane = lax.broadcasted_iota(jnp.int32, x.shape, 1)
    first, second, third = split3(x)
    picked = jnp.where(lane < count, first, jnp.where(lane < 2 * count, second, third))
    return jnp.where(lane < 3 * count, picked, 0.0).astype(BF16)


def head_slot(shape, count):
    slot = lax.broadcasted_iota(jnp.int32, shape, 0)
    live = slot < 3 * count
    slot = slot - jnp.where(slot >= 2 * count, 2 * count, jnp.where(slot >= count, count, 0))
    return jnp.where(live, slot, -1)


def spread_matrix(first_head, width, count):
    shape = (LANES, width)
    head = first_head + lax.broadcasted_iota(jnp.int32, shape, 1) // P_SIZE
    return jnp.where(head_slot(shape, count) == head, 1.0, 0.0).astype(BF16)


def dot(a, b):
    return jnp.dot(a, b, preferred_element_type=F32)


def near_kernel(inner_w, state_w, gate_w, near):
    near[...] = (
        inner_w[0:RIM, 0:LANES] + state_w[0:RIM, 0:LANES] + gate_w[0:RIM, 0:LANES]
    )


def tail_kernel(below, above, own, near, tail):
    here = lax.axis_index("head")
    last = [x[x.shape[0] - RIM :, :] for x in (below, above, own)]
    tail[...] = jnp.where(here == 0, last[0], jnp.where(here == 2, last[1], last[2]))


def repeat_lanes(x):
    count = x.shape[1]
    lane = lax.broadcasted_iota(jnp.int32, (count, LANES), 1)
    slot = lax.broadcasted_iota(jnp.int32, (count, LANES), 0)
    hits = (lane == slot) | (lane == slot + count) | (lane == slot + 2 * count)
    copies = jnp.where(hits, 1.0, 0.0).astype(BF16)
    return sum(dot(part.astype(BF16), copies) for part in split3(x))


def norm_rows(x, gain):
    x = x.astype(F32)
    mean = jnp.mean(x * x, axis=-1, keepdims=True)
    return (x * lax.rsqrt(mean + 1e-05) * gain).astype(BF16)


def project_kernel(
    own,
    below,
    above,
    top,
    bottom,
    gain,
    step_w,
    state_w,
    inner_w,
    gate_w,
    step_raw,
    state_raw,
    inner_raw,
    gate,
    normed,
):
    rows = own.shape[0]
    half = rows // 2
    here = lax.axis_index("head")

    def put(owner, offset, x):
        start = pl.multiple_of(owner * rows + offset, half)
        normed[pl.ds(start, x.shape[0]), :] = norm_rows(x[...], gain[...])

    far = (here + 2) % 4
    put(here, 0, own)
    put((here + 3) % 4, 0, below)
    put((here + 1) % 4, 0, above)
    put(far, 0, top)
    put(far, half, bottom)
    step_raw[...] = lax.dot_general(
        normed[...], step_w[...], (((1,), (1,)), ((), ())), preferred_element_type=F32
    )
    state_raw[...] = dot(normed[...], state_w[...]).astype(BF16)
    inner_raw[...] = dot(normed[...], inner_w[...]).astype(BF16)
    for c in range(gate.shape[1] // CHUNK):
        cols = slice(c * CHUNK, (c + 1) * CHUNK)
        vals = dot(normed[...], gate_w[:, cols]).astype(BF16).astype(F32)
        gate[:, cols] = vals * jax.nn.sigmoid(vals)


def block_kernel(
    lens_row,
    rim,
    rim_far,
    gain,
    step_raw,
    state_raw,
    inner_raw,
    step_bias,
    rate,
    taps_state,
    taps_inner,
    state_w,
    inner_w,
    sent,
    conv_out,
    scaled_out,
    cum_out,
    cum_rows,
    scores_out,
    maps_out,
    head_decay_out,
    local,
    *,
    heads_here,
):
    length = inner_raw.shape[0]
    first = lax.axis_index("seq") * length
    rim_rows = norm_rows(rim[...] + rim_far[...], gain[...])

    def behind(weight, raw):
        before = dot(rim_rows, weight[...]).astype(BF16).astype(F32)
        return jnp.concatenate([before, raw[...].astype(F32)], axis=0)

    passages = lens_row.shape[1]
    up = lax.broadcasted_iota(jnp.int32, (passages, passages), 0)
    across = lax.broadcasted_iota(jnp.int32, (passages, passages), 1)
    lens = jnp.broadcast_to(lens_row[...].astype(F32), (8, passages))
    whole = jnp.floor(lens * (1.0 / 128.0))
    before = jnp.where(up < across, 1.0, 0.0).astype(BF16)
    starts_row = 128.0 * dot(whole.astype(BF16), before)
    starts_row = (starts_row + dot((lens - 128.0 * whole).astype(BF16), before))[0:1]
    starts_col = jnp.sum(
        jnp.where(across < up, lens_row[...].astype(F32), 0.0), axis=1, keepdims=True
    )
    base = first.astype(F32)
    pos = lax.broadcasted_iota(jnp.int32, (length + RIM, passages), 0).astype(F32)
    ids_pad = jnp.sum(
        jnp.where(pos + (base - RIM) >= starts_row, 1.0, 0.0), axis=1, keepdims=True
    )
    pos = lax.broadcasted_iota(jnp.int32, (passages, length), 1).astype(F32)
    ids_row = jnp.sum(jnp.where(pos + base >= starts_col, 1.0, 0.0), axis=0, keepdims=True)
    ids_wide = jnp.broadcast_to(ids_pad, (length + RIM, LANES))
    ids = ids_wide[RIM:]
    agree = [
        jnp.where(pltpu.roll(ids_wide, lag, 0)[RIM:] == ids, 1.0, 0.0) for lag in range(1, K)
    ]

    def conv(raw, taps):
        acc = taps[0:1] * raw[RIM:]
        for lag in range(1, K):
            moved = pltpu.roll(raw, lag, 0)[RIM:]
            same = jnp.concatenate([agree[lag - 1]] * (raw.shape[1] // LANES), axis=1)
            acc = acc + taps[lag : lag + 1] * moved * same
        return (acc * jax.nn.sigmoid(acc)).astype(BF16)

    x = repeat_lanes(step_raw[...] + step_bias[...])
    rates = jnp.broadcast_to(rate[...].astype(F32) * 2.0 ** (-21), (8, rate.shape[1]))
    raw = behind(state_w, state_raw)
    maps = conv(raw, taps_state[...])
    maps_in = maps[:, :N]
    maps_out[...] = maps[:, N:]
    maps_in_t = maps_in.astype(F32).T.astype(BF16)
    t = lax.broadcasted_iota(jnp.int32, (length, length), 0)
    s = lax.broadcasted_iota(jnp.int32, (length, length), 1)
    ids_two = jnp.concatenate([ids] * (length // LANES), axis=1)
    mask = (ids_two == ids_row) & (t >= s)
    scores_out[...] = jnp.where(mask, dot(maps[:, N:], maps_in_t), 0.0)

    step = jnp.maximum(x, 0.0) + jnp.log1p(jnp.exp(-jnp.abs(x)))
    log_decay = -step * repeat_lanes(rates)[0:1]
    ones = jnp.where(t >= s, 1.0, 0.0).astype(BF16)
    cum = sum(dot(ones, part.astype(BF16)) for part in split3(log_decay))
    last = cum[length - 1 :, :]
    ids_last = ids[length - 1 :, :]
    prior = ids_wide[RIM - 1 : RIM, :]
    step3 = by_lane(step, heads_here)
    tail = jnp.exp(jnp.minimum(last - cum, 0.0)) * jnp.where(ids == ids_last, 1.0, 0.0)
    tail3 = by_lane(tail, heads_here)
    keep = jnp.exp(cum) * jnp.where(ids == prior, 1.0, 0.0)
    keep3 = by_lane(keep, heads_here)
    head_decay_out[...] = keep3
    cum_out[...] = by_lane(cum, heads_here)
    cum_rows[...] = cum.T

    raw = behind(inner_w, inner_raw)
    mixed = conv(raw, taps_inner[...])
    conv_out[...] = mixed
    spread = spread_matrix(0, local.shape[1], heads_here)
    scaled = (mixed.astype(F32) * dot(step3, spread)).astype(BF16)
    scaled_out[...] = scaled
    tail_in = (dot(tail3, spread) * scaled.astype(F32)).astype(BF16)
    local[...] = dot(maps_in_t, tail_in)

    span = local.shape[1] // 2
    decay = jnp.broadcast_to(keep3[length - RIM :].astype(F32)[RIM - 1 :], (8, LANES))
    for piece in range(sent.shape[0]):
        group, side = piece // 2, piece % 2
        part = local[8 * group : 8 * group + 8, side * span : (side + 1) * span]
        sent[piece, :, 0:span] = part.astype(BF16)
        sent[piece, :, span:] = decay.astype(BF16)


def inside_kernel(
    scaled,
    conv,
    cum,
    cum_rows,
    scores,
    skip,
    inside,
    *,
    heads_here,
):
    length = scaled.shape[0]
    half = length // 2
    per = CHUNK // P_SIZE
    lane = lax.broadcasted_iota(jnp.int32, (length, CHUNK), 1) // P_SIZE
    slots = head_slot((LANES, length), heads_here)
    skip3 = by_lane(repeat_lanes(jnp.broadcast_to(skip[...], (8, heads_here))), heads_here)
    for c in range(scaled.shape[1] // CHUNK):
        cols = slice(c * CHUNK, (c + 1) * CHUNK)
        x = scaled[:, cols]
        tops, bottoms, top_x, all_x = [], [], [], []
        for i in range(per):
            head = c * per + i
            pick = jnp.where(slots == head, 1.0, 0.0).astype(BF16)
            cum_t = dot(cum[...], pick)
            cum_s = cum_rows[head : head + 1, :]
            own = jnp.where(lane == i, x, jnp.zeros_like(x))
            upper = jnp.exp(jnp.minimum(cum_t[:half, :half] - cum_s[:, :half], 0.0))
            lower = jnp.exp(jnp.minimum(cum_t[half:] - cum_s, 0.0))
            tops.append((upper * scores[0:half, 0:half]).astype(BF16))
            bottoms.append((lower * scores[half:, :]).astype(BF16))
            top_x.append(own[:half])
            all_x.append(own)
        spread = spread_matrix(c * per, CHUNK, heads_here)
        skips = dot(skip3, spread)[0:1]
        upper = dot(jnp.concatenate(tops, axis=1), jnp.concatenate(top_x, axis=0))
        lower = dot(jnp.concatenate(bottoms, axis=1), jnp.concatenate(all_x, axis=0))
        inside[:, cols] = jnp.concatenate([upper, lower], axis=0) + (
            skips * conv[:, cols].astype(F32)
        )


def scan_kernel(got, back, *, heads_here):
    blocks, depth, width = got.shape
    span = width - LANES
    side = lax.axis_index("seq") % 2
    spread = spread_matrix(side * (span // P_SIZE), span, heads_here)
    parts = got[:, :, span:].astype(F32).reshape(blocks * depth, LANES).astype(BF16)
    decay = dot(parts, spread)
    state = jnp.zeros((depth, span), F32)
    for b in range(blocks):
        back[b] = state.astype(BF16)
        if b < blocks - 1:
            state = decay[b * depth : (b + 1) * depth] * state + got[b, :, 0:span].astype(F32)


def out_kernel(
    got,
    maps,
    head_decay,
    inside,
    gate,
    norm_gain,
    out_w,
    part,
    states,
    x,
    *,
    heads_here,
):
    length = inside.shape[0]
    span = got.shape[2]
    for piece in range(got.shape[0]):
        group, side = piece // 2, piece % 2
        states[8 * group : 8 * group + 8, side * span : (side + 1) * span] = got[piece].astype(
            F32
        )
    total = jnp.zeros((length, 1), F32)
    for c in range(inside.shape[1] // CHUNK):
        cols = slice(c * CHUNK, (c + 1) * CHUNK)
        spread = spread_matrix(c * (CHUNK // P_SIZE), CHUNK, heads_here)
        carried = dot(maps[...], states[:, cols].astype(BF16)) * dot(head_decay[...], spread)
        gated = (inside[:, cols] + carried) * gate[:, cols]
        total = total + jnp.sum(gated * gated, axis=1, keepdims=True)
        x[:, cols] = (gated * norm_gain[:, cols]).astype(BF16)
    width = out_w.shape[1]
    for c in range(width // WIDE):
        cols = slice(c * WIDE, (c + 1) * WIDE)
        part[:, cols] = dot(x[...], out_w[:, cols]).astype(BF16)
    part[:, width:] = by_lane(jnp.broadcast_to(total, (length, LANES)), 1)


def close_kernel(parts, mixed):
    rows, width = mixed.shape
    half = rows // 2
    for start in (0, half):
        total = sum(
            parts[peer * rows + start : peer * rows + start + half, :].astype(F32)
            for peer in range(parts.shape[0] // rows)
        )
        mean = jnp.sum(total[:, width:], axis=1, keepdims=True) / (H * P_SIZE)
        mixed[start : start + half, :] = (
            total[:, :width] * lax.rsqrt(mean + 1e-05)
        ).astype(BF16)


def vmem():
    return pl.BlockSpec(memory_space=pltpu.VMEM)


def call(kernel, name, in_specs, out_shape, scratch_shapes, limit):
    return pl.pallas_call(
        kernel,
        in_specs=in_specs,
        out_specs=[vmem()] * len(out_shape),
        out_shape=out_shape,
        scratch_shapes=scratch_shapes,
        compiler_params=pltpu.CompilerParams(vmem_limit_bytes=limit << 20),
        name=name,
    )


def on_device(
    tokens,
    input_gain,
    gate_weight,
    inner_weight,
    state_weight,
    step_weight,
    step_bias,
    decay_exponent,
    conv_inner,
    conv_state,
    skip_gain,
    norm_gain,
    out_weight,
    passage_lengths,
):
    rows, width = tokens.shape
    heads = lax.axis_size("head")
    blocks = lax.axis_size("seq")
    heads_here = step_weight.shape[1]
    channels = heads_here * P_SIZE
    length = heads * rows
    passages = passage_lengths.shape[0]
    span = channels // 2
    below, above, top, bottom, rim, rim_far = gather_tokens(
        tokens, inner_weight, state_weight, gate_weight
    )

    def shape(dims, kind):
        return jax.ShapeDtypeStruct(dims, kind)

    gain = input_gain[None]
    step_raw, state_raw, inner_raw, gate = call(
        project_kernel,
        "project",
        [vmem()] * 10,
        [
            shape((length, heads_here), F32),
            shape((length, 2 * N), BF16),
            shape((length, channels), BF16),
            shape((length, channels), F32),
        ],
        [pltpu.VMEM((length, width), BF16)],
        BLOCK_LIMIT,
    )(
        tokens,
        below,
        above,
        top,
        bottom,
        gain,
        step_weight.T,
        state_weight,
        inner_weight,
        gate_weight,
    )
    sent, conv, scaled, cum, cum_rows, scores, maps, head_decay = call(
        lambda *refs: block_kernel(*refs, heads_here=heads_here),
        "block",
        [vmem()] * 13,
        [
            shape((blocks, 8, span + LANES), BF16),
            shape((length, channels), BF16),
            shape((length, channels), BF16),
            shape((length, LANES), BF16),
            shape((LANES, length), F32),
            shape((length, length), F32),
            shape((length, N), BF16),
            shape((length, LANES), BF16),
        ],
        [pltpu.VMEM((N, channels), F32)],
        BLOCK_LIMIT,
    )(
        passage_lengths[None],
        rim,
        rim_far,
        gain,
        step_raw,
        state_raw,
        inner_raw,
        step_bias[None],
        decay_exponent[None],
        conv_state,
        conv_inner,
        state_weight,
        inner_weight,
    )

    (inside,) = call(
        lambda *refs: inside_kernel(*refs, heads_here=heads_here),
        "inside",
        [vmem()] * 6,
        [shape((length, channels), F32)],
        [],
        INSIDE_LIMIT,
    )(scaled, conv, cum, cum_rows, scores, skip_gain[None])
    sent, inside, gate, out_gain = lax.optimization_barrier(
        (sent, inside, gate, norm_gain[None])
    )
    got = lax.all_to_all(sent, "seq", 0, 0, tiled=True)

    (back,) = call(
        lambda *refs: scan_kernel(*refs, heads_here=heads_here),
        "scan",
        [vmem()],
        [shape((blocks, 8, span), BF16)],
        [],
        SMALL_LIMIT,
    )(got)
    states = lax.all_to_all(back, "seq", 0, 0, tiled=True)

    out_width = out_weight.shape[1]
    packed = out_width + LANES
    (part,) = call(
        lambda *refs: out_kernel(*refs, heads_here=heads_here),
        "out",
        [vmem()] * 7,
        [shape((length, packed), BF16)],
        [
            pltpu.VMEM((N, channels), F32),
            pltpu.VMEM((length, channels), BF16),
        ],
        OUT_LIMIT,
    )(states, maps, head_decay, inside, gate, out_gain, out_weight)
    (mixed,) = call(
        close_kernel,
        "close",
        [vmem()],
        [shape((rows, out_width), BF16)],
        [],
        SMALL_LIMIT,
    )(lax.all_to_all(part, "head", 0, 0, tiled=True))
    return mixed


def solution(mesh):
    in_specs = (
        P(("seq", "head"), None),
        P(),
        P(None, "head"),
        P(None, "head"),
        P(),
        P(None, "head"),
        P("head"),
        P("head"),
        P(None, "head"),
        P(),
        P("head"),
        P("head"),
        P("head", None),
        P(),
    )
    out_specs = P(("seq", "head"), None)
    return jax.shard_map(
        on_device, mesh=mesh, in_specs=in_specs, out_specs=out_specs, check_vma=False
    )
```
